32 devices in a mesh: row: 8 (over y, x, core), col: 4 (over z).
Axes of the slice: x: 2, y: 2, z: 4, core: 2. Of those that a mesh axis runs over, the one named last changes fastest.
Arguments:
- covariance: float32 [4096, 4096], P('row', 'col'), as said below
- phenotypes: float32 [4096, 512], P('row', 'col'), may hold values from -6 to 6
Outputs:
- updated: float32 [4096, 4096], P('row', 'col')
- solved: float32 [4096, 512], P(('row', 'col'))
The draws below stay inside these ranges and needn't reach their ends.
Inputs may be any that keep to these rules, and one draw needn't show every extreme that they name: covariance is symmetric and its leading 256 x 256 block is positive definite.
All inputs are finite; a program needn't handle non-finite values.
Results may differ from the reference program's by a relative error of at most 0.00007.
Values sent between devices are 32-bit elements; how exact they have to be, the bound alone decides.
No kernel may reach another device: no remote copies, remote signals or barrier semaphores. Data moves between devices by JAX's collectives and lax.ppermute only.
A program may use at most 64 MiB of HBM per device.

```python
import jax
import jax.numpy as jnp
from jax import lax

PANEL = 256
TRAITS = 512
ORDER = 4096


def draw_covariance(key, part):
    key_field = jax.random.fold_in(key, 11)
    key_diag = jax.random.fold_in(key, 23)
    uniform_field = jax.random.uniform(key_field, (ORDER, ORDER), jnp.float32, -1.0, 1.0)
    symmetric = 0.5 * (uniform_field + uniform_field.T)
    row_ids = lax.broadcasted_iota(jnp.int32, (ORDER, ORDER), 0)
    col_ids = lax.broadcasted_iota(jnp.int32, (ORDER, ORDER), 1)
    head_rows = row_ids < PANEL
    head_cols = col_ids < PANEL
    weights = jnp.where(head_rows | head_cols, 8.0, 1.0)
    levels = jax.random.uniform(key_diag, (ORDER,), jnp.float32, 0.0, 1.0)
    diag_values = 8.0 * (1.0 + levels)
    matrix = jnp.where(row_ids == col_ids, diag_values[:, None], symmetric * weights)
    block_rows = lax.broadcasted_iota(jnp.int32, (PANEL, PANEL), 0)
    block_cols = lax.broadcasted_iota(jnp.int32, (PANEL, PANEL), 1)
    distance = jnp.abs(block_rows - block_cols).astype(jnp.float32)
    decaying = jnp.exp(distance * jnp.log(jnp.float32(0.9)))
    head_diag = jnp.where(block_rows == block_cols, 0.8 * (1.0 + levels[:PANEL])[:, None], 0.0)
    head_block = 192.0 * (decaying + 0.003 * symmetric[:PANEL, :PANEL] + head_diag)
    matrix = lax.dynamic_update_slice(matrix, head_block.astype(jnp.float32), (0, 0))
    return matrix


def block_levels(rng, dims, cuts, least, high):
    factor_of = 1.0
    for axis_at, blocks in cuts:
        draws = jax.random.uniform(jax.random.fold_in(jax.random.fold_in(rng, 6), axis_at), (blocks,), jnp.float32, least / len(cuts), high / len(cuts))
        factor_of = factor_of * jnp.repeat(jnp.exp(draws), dims[axis_at] // blocks).reshape((-1,) + (1,) * (len(dims) - 1 - axis_at))
    return factor_of


def noise(rng, dims, scale, reach, split=(), kind=jnp.bfloat16):
    drawn = jax.random.normal(rng, dims, jnp.float32) * scale
    if len(split) > 0:
        drawn = block_levels(rng, dims, split, -0.22, 0.18) * drawn
    return jnp.clip(drawn, min=-reach, max=reach).astype(kind)


def setup_inputs(seed: int = 0) -> dict:
    keys = jax.random.split(jax.random.key(seed), 3)
    return {
        "covariance": draw_covariance(jax.random.fold_in(keys[2], 71), 0),
        "phenotypes": noise(keys[1], (ORDER, TRAITS), 1.0, 6.0, ((0, 8), (1, 4)), jnp.float32),
    }


EXACT_PRECISION = lax.Precision.HIGHEST

def invert_factor(matrix):
    factor = jnp.linalg.cholesky(matrix)
    identity = jnp.eye(matrix.shape[0], dtype=jnp.float32)
    return lax.linalg.triangular_solve(factor, identity, left_side=True, lower=True)

def reference(covariance, phenotypes):
    inverse = invert_factor(covariance[:PANEL, :PANEL])
    panel_rows = jnp.dot(covariance[:, :PANEL].astype(jnp.float32), inverse.T.astype(jnp.float32), precision=EXACT_PRECISION, preferred_element_type=jnp.float32)
    row_ids = lax.broadcasted_iota(jnp.int32, (ORDER, 1), 0)
    below = jnp.where(row_ids >= PANEL, panel_rows, jnp.zeros_like(panel_rows))
    product = lax.dot_general(below.astype(jnp.float32), below.astype(jnp.float32), (((1,), (1,)), ((), ())), precision=EXACT_PRECISION, preferred_element_type=jnp.float32)
    trailing = covariance - product
    updated = jnp.concatenate([panel_rows, trailing[:, PANEL:]], axis=1)
    head = jnp.dot(inverse.astype(jnp.float32), phenotypes[:PANEL].astype(jnp.float32), precision=EXACT_PRECISION, preferred_element_type=jnp.float32)
    remainder = phenotypes - jnp.dot(below.astype(jnp.float32), head.astype(jnp.float32), precision=EXACT_PRECISION, preferred_element_type=jnp.float32)
    solved = jnp.concatenate([head, remainder[PANEL:]], axis=0)
    return (updated, solved)
```

```python
import jax
import jax.numpy as jnp
from jax import lax
from jax.experimental import pallas as pl
from jax.experimental.pallas import tpu as pltpu
from jax.sharding import PartitionSpec as P

PANEL = 256
HALF = PANEL // 2
PIVOTS = 8
EXACT = lax.Precision.HIGHEST
AXES = ("row", "col")


def exact_dot(a, b, ca, cb):
    return lax.dot_general(
        a, b, (((ca,), (cb,)), ((), ())), precision=EXACT, preferred_element_type=jnp.float32
    )


def eliminate(t_ref, out_ref):
    n = t_ref.shape[0]
    shape = (PIVOTS, n)
    lane = lax.broadcasted_iota(jnp.int32, shape, 1)
    sub = lax.broadcasted_iota(jnp.int32, shape, 0)

    def spread(v, index):
        return jnp.take_along_axis(v, index, axis=1, mode="promise_in_bounds")

    def body(g, carry):
        k0 = g * PIVOTS
        base = pl.multiple_of(k0, PIVOTS)
        index = [jnp.full(shape, k0 + j, jnp.int32) for j in range(PIVOTS)]
        inside = (lane >= k0) & (lane < k0 + PIVOTS)
        pivot = t_ref[pl.ds(base, PIVOTS), :]
        columns = [spread(pivot, index[j]) for j in range(PIVOTS)]
        e = [
            [jnp.broadcast_to(columns[j][i : i + 1, :], shape) for j in range(i + 1)]
            for i in range(PIVOTS)
        ]
        r = []
        for k in range(PIVOTS):
            raw = jnp.broadcast_to(pivot[k : k + 1, :], shape)
            r.append(jnp.where(inside, jnp.where(lane == k0 + k, 1.0, 0.0), raw))
        inv = []
        low = [[None] * PIVOTS for _ in range(PIVOTS)]
        for k in range(PIVOTS):
            inv.append(1.0 / e[k][k])
            for i in range(k + 1, PIVOTS):
                low[i][k] = e[i][k] * inv[k]
                for j in range(k + 1, i + 1):
                    e[i][j] = e[i][j] - low[i][k] * e[j][k]
                r[i] = r[i] - low[i][k] * r[k]
        done = jnp.zeros(shape, jnp.float32)
        for k in range(PIVOTS):
            done = jnp.where(sub == k, r[k] * lax.rsqrt(e[k][k]), done)
        out_ref[pl.ds(base, PIVOTS), :] = jnp.where(lane < k0 + PIVOTS, done, 0.0)
        q = [r[k] * inv[k] for k in range(PIVOTS)]
        for k in range(PIVOTS - 1, 0, -1):
            for j in range(k):
                q[j] = q[j] - low[k][j] * q[k]
        for h in range(0, n, PIVOTS):
            row = t_ref[h : h + PIVOTS, :]
            acc = jnp.where(inside, 0.0, row)
            for j in range(PIVOTS):
                acc = acc - spread(row, index[j]) * q[j]
            t_ref[h : h + PIVOTS, :] = acc
        return carry

    lax.fori_loop(0, n // PIVOTS, body, 0)


def first_kernel(d_ref, w_ref, t_ref):
    t_ref[...] = d_ref[...]
    eliminate(t_ref, w_ref)


def second_kernel(d_ref, w11_ref, w_ref, t_ref, w22_ref):
    m = w11_ref.shape[0]
    n = d_ref.shape[1]
    w11 = w11_ref[...]
    l21 = exact_dot(d_ref[:, :m], w11, 1, 1)
    t_ref[...] = d_ref[:, m:] - exact_dot(l21, l21, 1, 1)
    below = exact_dot(l21, w11, 1, 0)
    eliminate(t_ref, w22_ref)
    w22 = w22_ref[...]
    w_ref[:m, :m] = w11
    w_ref[:m, m:] = jnp.zeros((m, n - m), jnp.float32)
    w_ref[m:, m:] = w22
    w_ref[m:, :m] = -exact_dot(w22, below, 1, 0)


def invert_first(d11):
    return pl.pallas_call(
        first_kernel,
        out_shape=jax.ShapeDtypeStruct(d11.shape, jnp.float32),
        scratch_shapes=[pltpu.VMEM(d11.shape, jnp.float32)],
        cost_estimate=pl.CostEstimate(flops=2_000_000_000, bytes_accessed=1 << 17, transcendentals=0),
    )(d11)


def invert_second(d_rest, w11):
    n = d_rest.shape[1]
    square = (n - w11.shape[0],) * 2
    return pl.pallas_call(
        second_kernel,
        out_shape=jax.ShapeDtypeStruct((n, n), jnp.float32),
        scratch_shapes=[pltpu.VMEM(square, jnp.float32), pltpu.VMEM(square, jnp.float32)],
        cost_estimate=pl.CostEstimate(flops=2_000_000_000, bytes_accessed=1 << 19, transcendentals=0),
    )(d_rest, w11)


def tree(nodes, level, levels, edges):
    if len(nodes) < 2:
        return
    half = len(nodes) // 2
    edges.append((level, levels[nodes[0]], nodes[0], nodes[half]))
    levels[nodes[half]] = level
    tree(nodes[:half], level + 1, levels, edges)
    tree(nodes[half:], level + 1, levels, edges)


def bit_reversed(count):
    bits = max(count - 1, 0).bit_length()
    order = [int(format(i, "0%db" % bits)[::-1], 2) if bits else 0 for i in range(1 << bits)]
    return [i for i in order if i < count]


def shards(covariance, phenotypes):
    rows_dev, cols_dev = covariance.shape
    row_size, col_size = lax.axis_size("row"), lax.axis_size("col")
    row_index, col_index = lax.axis_index("row"), lax.axis_index("col")
    ratio = row_size // col_size
    groups = row_size // ratio
    traits_dev = phenotypes.shape[1]

    def place(r, c):
        return r * col_size + c

    def send(x, pairs):
        return lax.ppermute(x, AXES, [(place(*a), place(*b)) for a, b in pairs])

    def run_tree(x, edges):
        stages = {}
        held = {0: x}
        total = None
        for level, source_level, a, b in edges:
            stages.setdefault((level, source_level), []).append((a, b))
        for key in sorted(stages):
            got = send(held[key[1]], stages[key])
            held[key[0]] = held[key[0]] + got if key[0] in held else got
            total = got if total is None else total + got
        return total

    at_root_row = row_index == 0
    at_root = at_root_row & (col_index == 0)

    def spread_diag(x):
        own = x
        got = None
        for c in range(1, col_size):
            y = send(own, [((0, 0), (0, c))])
            got = y if got is None else got + y
        x = jnp.where(at_root, own, got)
        got = None
        for k in range(1, groups):
            y = send(x, [((0, c), (k * ratio, c)) for c in range(col_size)])
            got = y if got is None else got + y
        x = jnp.where(at_root_row, x, got)
        got = None
        for m in range(1, ratio):
            y = send(x, [((k * ratio, c), (k * ratio + m, c)) for k in range(groups) for c in range(col_size)])
            got = y if got is None else got + y
        return jnp.where(lax.rem(row_index, ratio) == 0, x, got) if got is not None else x

    d11 = spread_diag(covariance[:HALF, :HALF])
    d_rest = spread_diag(covariance[HALF:PANEL, :PANEL])

    def row_edges(with_root):
        edges = []
        for r in range(row_size):
            if r == 0 and not with_root:
                continue
            nodes = [c for c in range(col_size) if c == 0 or c != r // ratio]
            found = []
            tree(nodes, 1, {0: 0}, found)
            edges += [(lv, sl, (r, a), (r, b)) for lv, sl, a, b in found]
        return edges

    rest_rows = run_tree(covariance[PANEL:, :PANEL], row_edges(True))
    top_rows = run_tree(covariance[:PANEL, :PANEL], row_edges(False))

    piece = cols_dev // ratio
    mine = None
    for m in range(ratio):
        slab = covariance[:PANEL, m * piece : (m + 1) * piece]
        nodes = list(range(groups)) if m % 2 == 0 else bit_reversed(groups)
        found = []
        tree(nodes, 1, {0: 0}, found)
        edges = []
        for lv, sl, a, b in found:
            source = (lambda c: (0, c)) if a == 0 else (lambda c, a=a: (a * ratio + m, c))
            edges += [(lv, sl, source(c), (b * ratio + m, c)) for c in range(col_size)]
        got = run_tree(slab, edges)
        if m:
            got = got + send(slab, [((0, c), (m, c)) for c in range(col_size)])
        mine = got if mine is None else mine + got
    own_slab = covariance[:PANEL, :piece]
    mine = jnp.where(at_root_row, own_slab, mine)
    member = lax.rem(row_index, ratio)
    slabs = [mine]
    for s in range(1, ratio):
        slabs.append(
            send(
                mine,
                [
                    ((k * ratio + m, c), (k * ratio + (m + s) % ratio, c))
                    for k in range(groups)
                    for m in range(ratio)
                    for c in range(col_size)
                ],
            )
        )
    ordered = []
    for m in range(ratio):
        block = slabs[0]
        for s in range(1, ratio):
            block = jnp.where(lax.rem(member - s + ratio, ratio) == m, slabs[s], block)
        ordered.append(block)
    panel_cols = jnp.concatenate(ordered, axis=1)

    head_rows = phenotypes[:PANEL]
    share = rows_dev // col_size
    head_parts = [head_rows]
    parts = [lax.dynamic_slice_in_dim(phenotypes, col_index * share, share, 0)]
    for s in range(1, col_size):
        head_parts.append(send(head_rows, [((0, c), (0, (c + s) % col_size)) for c in range(col_size)]))
        target = lax.rem(col_index + s, col_size)
        parts.append(
            send(
                lax.dynamic_slice_in_dim(phenotypes, target * share, share, 0),
                [((r, c), (r, (c + s) % col_size)) for r in range(row_size) for c in range(col_size)],
            )
        )

    def in_order(blocks):
        out = jnp.zeros((blocks[0].shape[0], col_size * traits_dev), jnp.float32)
        for s, block in enumerate(blocks):
            at = lax.rem(col_index - s + col_size, col_size) * traits_dev
            out = lax.dynamic_update_slice(out, block, (0, at))
        return out

    regrouped = in_order(parts)
    head_raw = in_order(head_parts)
    nodes = list(range(groups))
    found = []
    tree(nodes, 1, {0: 0}, found)
    edges = [
        (lv, sl, (a * ratio, c), (b * ratio, c)) for lv, sl, a, b in found for c in range(col_size)
    ]
    head_raw = jnp.where(at_root_row, head_raw, run_tree(head_raw, edges))
    got = None
    for m in range(1, ratio):
        y = send(
            head_raw,
            [((k * ratio, c), (k * ratio + m, c)) for k in range(groups) for c in range(col_size)],
        )
        got = y if got is None else got + y
    if got is not None:
        head_raw = jnp.where(member == 0, head_raw, got)

    group = row_index // ratio
    own_rows = covariance[:, :PANEL]
    arrived = jnp.concatenate([top_rows, rest_rows], axis=0)
    diag_full = None
    turned = lax.dynamic_slice_in_dim(panel_cols, member * rows_dev, rows_dev, 1).T
    panel_raw = jnp.where(
        col_index == 0, own_rows, jnp.where(col_index == group, turned, arrived)
    )

    w11 = invert_first(d11)
    inverse = invert_second(d_rest, w11)

    diag_full = jnp.concatenate(
        [jnp.concatenate([d11, d_rest[:, :HALF].T], axis=1), d_rest], axis=0
    )
    leading = jnp.where(at_root_row, diag_full, panel_raw[:PANEL])
    panel_raw = jnp.concatenate([leading, panel_raw[PANEL:]], axis=0)

    panel_rows = exact_dot(panel_raw, inverse, 1, 1)
    global_rows = row_index * rows_dev + lax.broadcasted_iota(jnp.int32, (rows_dev, 1), 0)
    below_rows = jnp.where(global_rows >= PANEL, panel_rows, 0.0)
    global_cols = col_index * cols_dev + lax.broadcasted_iota(jnp.int32, (1, cols_dev), 1)
    below_cols = jnp.where(global_cols >= PANEL, exact_dot(inverse, panel_cols, 1, 0), 0.0)
    trailing = covariance - exact_dot(below_rows, below_cols, 1, 0)
    first_part = jnp.where(col_index == 0, panel_rows, trailing[:, :PANEL])
    updated = jnp.concatenate([first_part, trailing[:, PANEL:]], axis=1)

    head_all = exact_dot(inverse, head_raw, 1, 0)
    offset = col_index * share
    my_factor = lax.dynamic_slice_in_dim(below_rows, offset, share, 0)
    computed = regrouped - exact_dot(my_factor, head_all, 1, 0)
    first_row = row_index * rows_dev + offset
    padded = jnp.concatenate(
        [head_all, jnp.zeros((share, head_all.shape[1]), jnp.float32)], axis=0
    )
    picked = lax.dynamic_slice_in_dim(padded, jnp.minimum(first_row, PANEL), share, 0)
    rows_here = first_row + lax.broadcasted_iota(jnp.int32, (share, 1), 0)
    solved = jnp.where(rows_here < PANEL, picked, computed)
    return (updated, solved)


def solution(mesh):
    placed = (P("row", "col"), P("row", "col"))
    return jax.shard_map(
        shards,
        mesh=mesh,
        in_specs=placed,
        out_specs=(P("row", "col"), P(("row", "col"), None)),
        check_vma=False,
    )
```

```python
import jax
import jax.numpy as jnp
from jax import lax
from jax.experimental import pallas as pl
from jax.experimental.pallas import tpu as pltpu
from jax.sharding import PartitionSpec as P

PANEL = 256
HALF = PANEL // 2
PIVOTS = 8
EXACT = lax.Precision.HIGHEST
AXES = ("row", "col")


def exact_dot(a, b, ca, cb):
    return lax.dot_general(
        a, b, (((ca,), (cb,)), ((), ())), precision=EXACT, preferred_element_type=jnp.float32
    )


def eliminate(t_ref, out_ref):
    n = t_ref.shape[0]
    shape = (PIVOTS, n)
    lane = lax.broadcasted_iota(jnp.int32, shape, 1)
    sub = lax.broadcasted_iota(jnp.int32, shape, 0)

    def spread(v, index):
        return jnp.take_along_axis(v, index, axis=1, mode="promise_in_bounds")

    def body(g, carry):
        k0 = g * PIVOTS
        base = pl.multiple_of(k0, PIVOTS)
        index = [jnp.full(shape, k0 + j, jnp.int32) for j in range(PIVOTS)]
        inside = (lane >= k0) & (lane < k0 + PIVOTS)
        pivot = t_ref[pl.ds(base, PIVOTS), :]
        columns = [spread(pivot, index[j]) for j in range(PIVOTS)]
        e = [
            [jnp.broadcast_to(columns[j][i : i + 1, :], shape) for j in range(i + 1)]
            for i in range(PIVOTS)
        ]
        r = []
        for k in range(PIVOTS):
            raw = jnp.broadcast_to(pivot[k : k + 1, :], shape)
            r.append(jnp.where(inside, jnp.where(lane == k0 + k, 1.0, 0.0), raw))
        inv = []
        low = [[None] * PIVOTS for _ in range(PIVOTS)]
        for k in range(PIVOTS):
            inv.append(1.0 / e[k][k])
            for i in range(k + 1, PIVOTS):
                low[i][k] = e[i][k] * inv[k]
                for j in range(k + 1, i + 1):
                    e[i][j] = e[i][j] - low[i][k] * e[j][k]
                r[i] = r[i] - low[i][k] * r[k]
        done = jnp.zeros(shape, jnp.float32)
        for k in range(PIVOTS):
            done = jnp.where(sub == k, r[k] * lax.rsqrt(e[k][k]), done)
        out_ref[pl.ds(base, PIVOTS), :] = jnp.where(lane < k0 + PIVOTS, done, 0.0)
        q = [r[k] * inv[k] for k in range(PIVOTS)]
        for k in range(PIVOTS - 1, 0, -1):
            for j in range(k):
                q[j] = q[j] - low[k][j] * q[k]
        for h in range(0, n, PIVOTS):
            row = t_ref[h : h + PIVOTS, :]
            acc = jnp.where(inside, 0.0, row)
            for j in range(PIVOTS):
                acc = acc - spread(row, index[j]) * q[j]
            t_ref[h : h + PIVOTS, :] = acc
        return carry

    lax.fori_loop(0, n // PIVOTS, body, 0)


def factor_kernel(d_ref, w_ref, t_ref, w11_ref, w22_ref):
    m = d_ref.shape[0]
    t_ref[...] = d_ref[:, :m]
    eliminate(t_ref, w11_ref)
    w11 = w11_ref[...]
    l21 = exact_dot(d_ref[:, m : 2 * m], w11, 1, 1)
    t_ref[...] = d_ref[:, 2 * m :] - exact_dot(l21, l21, 1, 1)
    below = exact_dot(l21, w11, 1, 0)
    eliminate(t_ref, w22_ref)
    w22 = w22_ref[...]
    w_ref[:, :m] = w11
    w_ref[:, m : 2 * m] = -exact_dot(w22, below, 1, 0)
    w_ref[:, 2 * m :] = w22


def factor_inverse(blocks):
    m = blocks.shape[0]
    return pl.pallas_call(
        factor_kernel,
        out_shape=jax.ShapeDtypeStruct(blocks.shape, jnp.float32),
        scratch_shapes=[pltpu.VMEM((m, m), jnp.float32)] * 3,
        cost_estimate=pl.CostEstimate(flops=1 << 33, bytes_accessed=1 << 19, transcendentals=0),
    )(blocks)


def full_inverse(w_ref, out_ref):
    m = w_ref.shape[0]
    out_ref[:m, :m] = w_ref[:, :m]
    out_ref[:m, m:] = jnp.zeros((m, m), jnp.float32)
    out_ref[m:, :] = w_ref[:, m:]


def solve_kernel(col_size, w_ref, rows_ref, head_ref, pheno_ref, panel_ref, *rest):
    part_refs, (inv_ref, left_ref) = rest[:col_size], rest[col_size:]
    row, col = lax.axis_index("row"), lax.axis_index("col")
    full_inverse(w_ref, inv_ref)
    inverse = inv_ref[...]
    panel = exact_dot(rows_ref[...], inverse, 1, 1)
    panel_ref[...] = panel
    head = exact_dot(inverse, head_ref[...], 1, 0)
    left_ref[...] = pheno_ref[...] - exact_dot(panel, head, 1, 0)

    @pl.when(row == 0)
    def _():
        left_ref[:PANEL, :] = head

    share = left_ref.shape[0] // col_size
    for s in range(col_size):
        at = pl.multiple_of(lax.rem(col + s, col_size) * share, share)
        part_refs[s][...] = left_ref[pl.ds(at, share), :]


def solve_rows(blocks, rows, head, pheno, col_size):
    n = rows.shape[0]
    part = jax.ShapeDtypeStruct((n // col_size, pheno.shape[1]), jnp.float32)
    return pl.pallas_call(
        lambda *refs: solve_kernel(col_size, *refs),
        out_shape=[jax.ShapeDtypeStruct(rows.shape, jnp.float32)] + [part] * col_size,
        scratch_shapes=[
            pltpu.VMEM((PANEL, PANEL), jnp.float32),
            pltpu.VMEM(pheno.shape, jnp.float32),
        ],
        cost_estimate=pl.CostEstimate(flops=1 << 30, bytes_accessed=1 << 21, transcendentals=0),
    )(blocks, rows, head, pheno)


def trailing_kernel(w_ref, panel_ref, cols_ref, cov_ref, out_ref, inv_ref, below_ref):
    row, col = lax.axis_index("row"), lax.axis_index("col")
    step = pl.program_id(0)

    @pl.when(step == 0)
    def _():
        full_inverse(w_ref, inv_ref)
        below_ref[...] = panel_ref[...]

        @pl.when(row == 0)
        def _():
            below_ref[:PANEL, :] = jnp.zeros((PANEL, PANEL), jnp.float32)

    right = exact_dot(inv_ref[...], cols_ref[...], 1, 0)
    out_ref[...] = cov_ref[...] - exact_dot(below_ref[...], right, 1, 0)

    @pl.when((col == 0) & (step == 0))
    def _():
        out_ref[...] = panel_ref[...]


def trailing_update(blocks, panel, cols, covariance):
    n, width = covariance.shape
    return pl.pallas_call(
        trailing_kernel,
        grid=(width // PANEL,),
        in_specs=[
            pl.BlockSpec(blocks.shape, lambda j: (0, 0)),
            pl.BlockSpec(panel.shape, lambda j: (0, 0)),
            pl.BlockSpec((PANEL, PANEL), lambda j: (0, j)),
            pl.BlockSpec((n, PANEL), lambda j: (0, j)),
        ],
        out_specs=pl.BlockSpec((n, PANEL), lambda j: (0, j)),
        out_shape=jax.ShapeDtypeStruct(covariance.shape, jnp.float32),
        scratch_shapes=[
            pltpu.VMEM((PANEL, PANEL), jnp.float32),
            pltpu.VMEM((n, PANEL), jnp.float32),
        ],
        cost_estimate=pl.CostEstimate(flops=1 << 31, bytes_accessed=6 << 20, transcendentals=0),
    )(blocks, panel, cols, covariance)


def tree(nodes, level, levels, edges):
    if len(nodes) < 2:
        return
    half = len(nodes) // 2
    edges.append((level, levels[nodes[0]], nodes[0], nodes[half]))
    levels[nodes[half]] = level
    tree(nodes[:half], level + 1, levels, edges)
    tree(nodes[half:], level + 1, levels, edges)


def bit_reversed(count):
    bits = max(count - 1, 0).bit_length()
    order = [int(format(i, "0%db" % bits)[::-1], 2) if bits else 0 for i in range(1 << bits)]
    return [i for i in order if i < count]


def choose(index, options):
    out = options[0]
    for i in range(1, len(options)):
        out = jnp.where(index == i, options[i], out)
    return out


def shards(covariance, phenotypes):
    rows_dev, cols_dev = covariance.shape
    row_size, col_size = lax.axis_size("row"), lax.axis_size("col")
    row_index, col_index = lax.axis_index("row"), lax.axis_index("col")
    ratio = row_size // col_size
    groups = row_size // ratio
    traits_dev = phenotypes.shape[1]
    group, member = row_index // ratio, lax.rem(row_index, ratio)

    def place(r, c):
        return r * col_size + c

    def send(x, pairs):
        to = {place(*a): place(*b) for a, b in pairs}
        count = row_size * col_size
        taken = set(to.values())
        for a, b in list(to.items()):
            if b not in to and a not in taken:
                to[b] = a
                taken.add(a)
        for r in range(row_size):
            for c in range(col_size):
                a = place(r, c)
                for m in range(1, ratio):
                    b = place(r // ratio * ratio + (r + m) % ratio, c)
                    if a not in to and b not in taken:
                        to[a] = b
                        taken.add(b)
        for a in range(count):
            if a not in to and a not in taken:
                to[a] = a
                taken.add(a)
        free = [b for b in range(count) if b not in taken]
        for a in range(count):
            if a not in to:
                to[a] = free.pop()
        return lax.ppermute(x, AXES, sorted(to.items()))

    every_group = [(k, c) for k in range(groups) for c in range(col_size)]

    blocks = jnp.concatenate(
        [covariance[:HALF, :HALF], covariance[HALF:PANEL, :HALF], covariance[HALF:PANEL, HALF:PANEL]],
        axis=1,
    )
    diag = [blocks] + [send(blocks, [((0, 0), (0, c))]) for c in range(1, col_size)]
    diag = choose(col_index, diag)

    piece = cols_dev // ratio
    head_share = PANEL // ratio
    across = piece // traits_dev
    head_rows = head_share // across

    def payload(m):
        head = phenotypes[m * head_share : (m + 1) * head_share]
        head = jnp.concatenate([head[i * head_rows : (i + 1) * head_rows] for i in range(across)], axis=1)
        return jnp.concatenate([covariance[:PANEL, m * piece : (m + 1) * piece], head], axis=0)

    own_payload = payload(0)
    start = [own_payload]
    for m in range(1, ratio):
        start.append(send(payload(m), [((0, c), (m, c)) for c in range(col_size)]))
    start = choose(row_index, start) if ratio > 1 else own_payload
    edges = []
    for m in range(ratio):
        nodes = list(range(groups)) if m % 2 == 0 else bit_reversed(groups)
        found = []
        tree(nodes, 1, {0: 0}, found)
        edges += [(lv, sl, a * ratio + m, b * ratio + m) for lv, sl, a, b in found]
    stages = {}
    came = {}
    for lv, sl, a, b in edges:
        stages.setdefault((lv, sl), []).append((a, b))
        came[b] = (lv, sl)
    keys = sorted(stages)
    results = [start]
    held = {0: start}
    for key in keys:
        pairs = [((a, c), (b, c)) for a, b in stages[key] for c in range(col_size)]
        got = send(held[key[1]], pairs)
        results.append(got)
        if key[0] in held:
            here = [r for r in range(row_size) if came.get(r) == key]
            mask = sum((row_index == r).astype(jnp.int32) for r in here) > 0
            held[key[0]] = jnp.where(mask, got, held[key[0]])
        else:
            held[key[0]] = got
    source = sum(jnp.where(row_index == r, int(keys.index(came[r]) + 1 if r in came else 0), 0) for r in range(row_size))
    mine = choose(source, results)

    own_rows = covariance[:, :PANEL]
    targets = [[c for c in range(1, col_size) if c != r // ratio] for r in range(row_size)]
    arrived = []
    for j in range(col_size - 1):
        arrived.append(
            send(own_rows, [((r, 0), (r, targets[r][j])) for r in range(row_size) if len(targets[r]) > j])
        )

    inverse = lax.cond(row_index == 0, factor_inverse, lambda d: d, diag)

    others = [mine]
    for s in range(1, ratio):
        others.append(
            send(mine, [((k * ratio + m, c), (k * ratio + (m + s) % ratio, c)) for k, c in every_group for m in range(ratio)])
        )
    ordered = [choose(lax.rem(member - m + ratio, ratio), others) for m in range(ratio)]
    panel_cols = jnp.concatenate([x[:PANEL] for x in ordered], axis=1)
    head_raw = jnp.concatenate(
        [x[PANEL:, i * traits_dev : (i + 1) * traits_dev] for x in ordered for i in range(across)], axis=0
    )

    order = jnp.where(col_index > group, col_index - 1, col_index)
    order = jnp.where(group == 0, col_index, order)
    turned = mine[:PANEL].T
    panel_raw = choose(
        jnp.where(col_index == 0, 0, jnp.where(col_index == group, col_size, order)),
        [own_rows] + arrived + [turned],
    )

    got = [inverse]
    for k in range(1, groups):
        got.append(send(inverse, [((0, c), (k * ratio, c)) for c in range(col_size)]))
    inverse = choose(group, got)
    got = [inverse]
    for m in range(1, ratio):
        got.append(send(inverse, [((k * ratio, c), (k * ratio + m, c)) for k, c in every_group]))
    inverse = choose(member, got)

    panel, *parts = solve_rows(inverse, panel_raw, head_raw, phenotypes, col_size)
    gathered = [parts[0]]
    for s in range(1, col_size):
        gathered.append(
            send(parts[s], [((r, c), (r, (c + s) % col_size)) for r in range(row_size) for c in range(col_size)])
        )
    updated = trailing_update(inverse, panel, panel_cols, covariance)
    solved = jnp.concatenate(
        [choose(lax.rem(col_index - p + col_size, col_size), gathered) for p in range(col_size)], axis=1
    )
    return (updated, solved)


def solution(mesh):
    placed = (P("row", "col"), P("row", "col"))
    return jax.shard_map(
        shards,
        mesh=mesh,
        in_specs=placed,
        out_specs=(P("row", "col"), P(("row", "col"), None)),
        check_vma=False,
    )
```

```python
import jax
import jax.numpy as jnp
from jax import lax
from jax.experimental import pallas as pl
from jax.experimental.pallas import tpu as pltpu
from jax.sharding import PartitionSpec as P


PANEL = 256
HALF = PANEL // 2
PIVOTS = 8
EXACT = lax.Precision.HIGHEST
AXES = ("row", "col")


def exact_dot(a, b, ca, cb):
    return lax.dot_general(
        a, b, (((ca,), (cb,)), ((), ())), precision=EXACT, preferred_element_type=jnp.float32
    )


def split(x, terms):
    out = []
    for _ in range(terms):
        out.append(x.astype(jnp.bfloat16))
        x = x - out[-1].astype(jnp.float32)
    return out


def split_dot(a, b, ca, cb):
    total = None
    for order in reversed(range(len(a))):
        for i in range(order + 1):
            part = lax.dot_general(
                a[i], b[order - i], (((ca,), (cb,)), ((), ())), preferred_element_type=jnp.float32
            )
            total = part if total is None else total + part
    return total


def eliminate(block, out_ref):
    n = block.shape[0]
    shape = (PIVOTS, n)
    lane = lax.broadcasted_iota(jnp.int32, shape, 1)
    sub = lax.broadcasted_iota(jnp.int32, shape, 0)
    steps = n // PIVOTS

    def spread(x, k):
        return jnp.broadcast_to(x[:, k : k + 1], shape)

    def row_of(x, i):
        return jnp.broadcast_to(x[i : i + 1, :], shape)

    t = [block[PIVOTS * h : PIVOTS * (h + 1), :] for h in range(steps)]
    pivots = [spread(t[0], j) for j in range(PIVOTS)]
    for g in range(steps):
        k0 = g * PIVOTS
        more = g + 1 < steps
        inside = (lane >= k0) & (lane < k0 + PIVOTS)
        e = [[row_of(pivots[j], i) for j in range(i + 1)] for i in range(PIVOTS)]
        r = [
            jnp.where(inside, jnp.where(lane == k0 + k, 1.0, 0.0), row_of(t[g], k))
            for k in range(PIVOTS)
        ]
        if more:
            c = [spread(t[g + 1], k0 + j) for j in range(PIVOTS)]
            following = [spread(t[g + 1], k0 + PIVOTS + j) for j in range(PIVOTS)]
            rows = jnp.where(inside, 0.0, t[g + 1])
        inv = []
        low = [[None] * PIVOTS for _ in range(PIVOTS)]
        for k in range(PIVOTS):
            inv.append(1.0 / e[k][k])
            for i in range(k + 1, PIVOTS):
                low[i][k] = e[i][k] * inv[k]
                for j in range(k + 1, i + 1):
                    e[i][j] = e[i][j] - low[i][k] * e[j][k]
                r[i] = r[i] - low[i][k] * r[k]
            if more:
                f = c[k] * inv[k]
                for j in range(k + 1, PIVOTS):
                    c[j] = c[j] - f * e[j][k]
                rows = rows - f * r[k]
                for j in range(PIVOTS):
                    following[j] = following[j] - f * row_of(c[k], j)
        done = jnp.zeros(shape, jnp.float32)
        for k in range(PIVOTS):
            done = jnp.where(sub == k, r[k] * lax.rsqrt(e[k][k]), done)
        out_ref[k0 : k0 + PIVOTS, :] = jnp.where(lane < k0 + PIVOTS, done, 0.0)
        if not more:
            break
        t[g + 1] = rows
        pivots = following
        if g + 2 < steps:
            q = [r[k] * inv[k] for k in range(PIVOTS)]
            for k in range(PIVOTS - 1, 0, -1):
                for j in range(k):
                    q[j] = q[j] - low[k][j] * q[k]
            for h in range(g + 2, steps):
                acc = jnp.where(inside, 0.0, t[h])
                for j in range(PIVOTS):
                    acc = acc - spread(t[h], k0 + j) * q[j]
                t[h] = acc


def factor_kernel(d_ref, w_ref, w11_ref, w22_ref):
    m = d_ref.shape[0]
    eliminate(d_ref[:, :m], w11_ref)
    w11 = w11_ref[...]
    l21 = exact_dot(d_ref[:, m : 2 * m], w11, 1, 1)
    rest = d_ref[:, 2 * m :] - exact_dot(l21, l21, 1, 1)
    below = exact_dot(l21, w11, 1, 0)
    eliminate(rest, w22_ref)
    w22 = w22_ref[...]
    w_ref[:, :m] = w11
    w_ref[:, m : 2 * m] = -exact_dot(w22, below, 1, 0)
    w_ref[:, 2 * m :] = w22


def factor_inverse(blocks):
    m = blocks.shape[0]
    return pl.pallas_call(
        factor_kernel,
        out_shape=jax.ShapeDtypeStruct(blocks.shape, jnp.float32),
        scratch_shapes=[pltpu.VMEM((m, m), jnp.float32)] * 2,
        cost_estimate=pl.CostEstimate(flops=1 << 32, bytes_accessed=1 << 19, transcendentals=0),
    )(blocks)


def full_inverse(w_ref, out_ref):
    m = w_ref.shape[0]
    out_ref[:m, :m] = w_ref[:, :m]
    out_ref[:m, m:] = jnp.zeros((m, m), jnp.float32)
    out_ref[m:, :] = w_ref[:, m:]


def solve_kernel(col_size, ratio, *refs):
    w_ref, rows_ref, pheno_ref = refs[:3]
    lead_refs = refs[3 : 3 + ratio]
    panel_ref = refs[3 + ratio]
    part_refs = refs[4 + ratio : 4 + ratio + col_size]
    inv_ref, head_ref, left_ref = refs[4 + ratio + col_size :]
    row, col = lax.axis_index("row"), lax.axis_index("col")
    member = lax.rem(row, ratio)
    head_share = PANEL // ratio
    traits = head_ref.shape[1]
    for s in range(ratio):
        first = lax.rem(member - s + ratio, ratio) * head_share
        height, width = lead_refs[s].shape
        for i in range(width // traits):
            at = pl.multiple_of(first + i * height, 8)
            head_ref[pl.ds(at, height), :] = lead_refs[s][:, i * traits : (i + 1) * traits]
    full_inverse(w_ref, inv_ref)
    inverse = split(inv_ref[...], 3)
    head = split_dot(inverse, split(head_ref[...], 3), 1, 0)
    panel = split_dot(split(rows_ref[...], 3), inverse, 1, 1)
    panel_ref[...] = panel
    left_ref[...] = pheno_ref[...] - split_dot(split(panel, 2), split(head, 2), 1, 0)

    @pl.when(row == 0)
    def _():
        left_ref[:PANEL, :] = head

    share = left_ref.shape[0] // col_size
    for s in range(col_size):
        at = pl.multiple_of(lax.rem(col + s, col_size) * share, share)
        part_refs[s][...] = left_ref[pl.ds(at, share), :]


def whole(shape):
    return pl.BlockSpec(shape, lambda *_: (0,) * len(shape))


def solve_rows(blocks, rows, pheno, slabs, col_size):
    n, traits = pheno.shape
    ratio = len(slabs)
    height = slabs[0].shape[0] - PANEL
    part = jax.ShapeDtypeStruct((n // col_size, traits), jnp.float32)
    lead = pl.BlockSpec((height, slabs[0].shape[1]), lambda *_: (PANEL // height, 0))
    outs = [jax.ShapeDtypeStruct(rows.shape, jnp.float32)] + [part] * col_size
    return pl.pallas_call(
        lambda *refs: solve_kernel(col_size, ratio, *refs),
        grid=(1,),
        in_specs=[whole(blocks.shape), whole(rows.shape), whole(pheno.shape)] + [lead] * ratio,
        out_specs=[whole(o.shape) for o in outs],
        out_shape=outs,
        scratch_shapes=[
            pltpu.VMEM((PANEL, PANEL), jnp.float32),
            pltpu.VMEM((PANEL, traits), jnp.float32),
            pltpu.VMEM(pheno.shape, jnp.float32),
        ],
        cost_estimate=pl.CostEstimate(flops=1 << 30, bytes_accessed=1 << 21, transcendentals=0),
    )(blocks, rows, pheno, *slabs)


def trailing_kernel(ratio, *refs):
    w_ref, panel_ref, cov_ref = refs[:3]
    slab_refs = refs[3 : 3 + ratio]
    out_ref, inv_ref, high_ref, low_ref = refs[3 + ratio :]
    row, col = lax.axis_index("row"), lax.axis_index("col")
    member = lax.rem(row, ratio)
    step = pl.program_id(0)

    @pl.when(step == 0)
    def _():
        full_inverse(w_ref, inv_ref)
        inverse = split(inv_ref[...], 3)
        for s in range(ratio):
            piece = slab_refs[s].shape[1]
            first = lax.rem(member - s + ratio, ratio) * piece
            for h in range(0, piece, PANEL):
                right = split_dot(inverse, split(slab_refs[s][:, h : h + PANEL], 3), 1, 0)
                at = pl.ds(pl.multiple_of(first + h, PANEL), PANEL)
                high_ref[:, at], low_ref[:, at] = split(right, 2)

    panel = panel_ref[...]
    lead = (row == 0) & (step * panel.shape[0] < PANEL)
    below = jnp.where(lead, 0.0, panel)
    right = [high_ref[...], low_ref[...]]
    out_ref[...] = cov_ref[...] - split_dot(split(below, 2), right, 1, 0)

    @pl.when(col == 0)
    def _():
        out_ref[:, :PANEL] = panel


def trailing_update(blocks, panel, covariance, slabs):
    n, width = covariance.shape
    ratio = len(slabs)
    tall = min(n, PANEL)
    slab = pl.BlockSpec((PANEL, slabs[0].shape[1]), lambda i: (0, 0))
    return pl.pallas_call(
        lambda *refs: trailing_kernel(ratio, *refs),
        grid=(n // tall,),
        in_specs=[
            whole(blocks.shape),
            pl.BlockSpec((tall, PANEL), lambda i: (i, 0)),
            pl.BlockSpec((tall, width), lambda i: (i, 0)),
        ]
        + [slab] * ratio,
        out_specs=pl.BlockSpec((tall, width), lambda i: (i, 0)),
        out_shape=jax.ShapeDtypeStruct(covariance.shape, jnp.float32),
        scratch_shapes=[
            pltpu.VMEM((PANEL, PANEL), jnp.float32),
            pltpu.VMEM((PANEL, width), jnp.bfloat16),
            pltpu.VMEM((PANEL, width), jnp.bfloat16),
        ],
        cost_estimate=pl.CostEstimate(flops=1 << 31, bytes_accessed=6 << 20, transcendentals=0),
    )(blocks, panel, covariance, *slabs)


def tree(nodes, level, levels, edges):
    if len(nodes) < 2:
        return
    half = len(nodes) // 2
    edges.append((level, levels[nodes[0]], nodes[0], nodes[half]))
    levels[nodes[half]] = level
    tree(nodes[:half], level + 1, levels, edges)
    tree(nodes[half:], level + 1, levels, edges)


def bit_reversed(count):
    bits = max(count - 1, 0).bit_length()
    order = [int(format(i, "0%db" % bits)[::-1], 2) if bits else 0 for i in range(1 << bits)]
    return [i for i in order if i < count]


def choose(index, options):
    out = options[0]
    for i in range(1, len(options)):
        out = jnp.where(index == i, options[i], out)
    return out


def look_up(table, *at):
    table = jnp.asarray(table, jnp.int32)
    return lax.dynamic_slice(table, at, (1,) * table.ndim).reshape(())


def shards(covariance, phenotypes):
    _, cols_dev = covariance.shape
    row_size, col_size = lax.axis_size("row"), lax.axis_size("col")
    row_index, col_index = lax.axis_index("row"), lax.axis_index("col")
    ratio = row_size // col_size
    groups = row_size // ratio
    traits_dev = phenotypes.shape[1]
    group, member = row_index // ratio, lax.rem(row_index, ratio)

    def place(r, c):
        return r * col_size + c

    def send(x, pairs):
        return lax.ppermute(x, AXES, [(place(*a), place(*b)) for a, b in pairs])

    every_group = [(k, c) for k in range(groups) for c in range(col_size)]

    blocks = jnp.concatenate(
        [covariance[:HALF, :HALF], covariance[HALF:PANEL, :HALF], covariance[HALF:PANEL, HALF:PANEL]],
        axis=1,
    )
    diag = [blocks]
    for c in range(1, col_size):
        diag.append(send(blocks, [((0, 0), (0, c))]))
    diag = choose(col_index, diag)

    piece = cols_dev // ratio
    head_share = PANEL // ratio
    across = piece // traits_dev
    head_rows = head_share // across
    tied, tied_pheno, _ = lax.optimization_barrier((covariance, phenotypes, blocks))

    def payload(m):
        head = tied_pheno[m * head_share : (m + 1) * head_share]
        head = jnp.concatenate([head[i * head_rows : (i + 1) * head_rows] for i in range(across)], axis=1)
        return jnp.concatenate([tied[:PANEL, m * piece : (m + 1) * piece], head], axis=0)

    start = [payload(0)]
    for m in range(1, ratio):
        start.append(send(payload(m), [((0, c), (m, c)) for c in range(col_size)]))
    start = choose(row_index, start)
    stages = {}
    came = {}
    for m in range(ratio):
        nodes = list(range(groups)) if m % 2 == 0 else bit_reversed(groups)
        found = []
        tree(nodes, 1, {0: 0}, found)
        for lv, sl, a, b in found:
            stages.setdefault((lv, sl), []).append((a * ratio + m, b * ratio + m))
            came[b * ratio + m] = (lv, sl)
    keys = sorted(stages)
    results = [start]
    held = {0: start}
    for key in keys:
        pairs = [((a, c), (b, c)) for a, b in stages[key] for c in range(col_size)]
        got = send(held[key[1]], pairs)
        results.append(got)
        if key[0] in held:
            here = [int(came.get(r) == key) for r in range(row_size)]
            held[key[0]] = jnp.where(look_up(here, row_index) > 0, got, held[key[0]])
        else:
            held[key[0]] = got
    source = look_up([keys.index(came[r]) + 1 if r in came else 0 for r in range(row_size)], row_index)

    own_rows = tied[:, :PANEL]
    relay_from = col_size // 2
    table = [[0] * col_size for _ in range(row_size)]
    targets = []
    for r in range(row_size):
        k = r // ratio
        if k:
            line = [c for c in range(1, col_size) if c != k]
        else:
            line = [relay_from] + [c for c in range(1, col_size - 1) if c != relay_from]
        targets.append(line)
        for j, c in enumerate(line):
            table[r][c] = j + 1
        if k:
            table[r][k] = col_size
        else:
            table[r][col_size - 1] = col_size - 1
    arrived = []
    for j in range(col_size - 2):
        arrived.append(send(own_rows, [((r, 0), (r, targets[r][j])) for r in range(row_size) if j < len(targets[r])]))

    inverse = factor_inverse(diag)
    got = [inverse]
    for k in range(1, groups):
        got.append(send(inverse, [((0, c), (k * ratio, c)) for c in range(col_size)]))
    inverse = choose(group, got)

    arrived.append(send(arrived[0], [((r, relay_from), (r, col_size - 1)) for r in range(ratio)]))
    mine = choose(source, results)
    slabs = [mine]
    for s in range(1, ratio):
        slabs.append(
            send(
                mine,
                [((k * ratio + m, c), (k * ratio + (m + s) % ratio, c)) for k, c in every_group for m in range(ratio)],
            )
        )

    turned = mine[:PANEL].T
    panel_raw = choose(look_up(table, row_index, col_index), [own_rows] + arrived + [turned])

    got = [inverse]
    for m in range(1, ratio):
        got.append(send(inverse, [((k * ratio, c), (k * ratio + m, c)) for k, c in every_group]))
    inverse = choose(member, got)

    panel, *parts = solve_rows(inverse, panel_raw, phenotypes, slabs, col_size)
    gathered = [parts[0]]
    for s in range(1, col_size):
        gathered.append(
            send(parts[s], [((r, c), (r, (c + s) % col_size)) for r in range(row_size) for c in range(col_size)])
        )
    updated = trailing_update(inverse, panel, covariance, slabs)
    solved = jnp.concatenate(
        [choose(lax.rem(col_index - p + col_size, col_size), gathered) for p in range(col_size)], axis=1
    )
    return (updated, solved)


def solution(mesh):
    placed = (P("row", "col"), P("row", "col"))

    return jax.shard_map(
        shards,
        mesh=mesh,
        in_specs=placed,
        out_specs=(P("row", "col"), P(("row", "col"), None)),
        check_vma=False,
    )
```

```python
import jax
import jax.numpy as jnp
from jax import lax
from jax.experimental import pallas as pl
from jax.experimental.pallas import tpu as pltpu
from jax.sharding import PartitionSpec as P


PANEL = 256
HALF = PANEL // 2
PIVOTS = 8
EXACT = lax.Precision.HIGHEST
AXES = ("row", "col")


MIB = 1 << 20
ANYWHERE = pl.BlockSpec(memory_space=pl.ANY)
IN_PLACE = pl.BlockSpec(memory_space=pltpu.HBM)


def grant(mib):
    return pltpu.CompilerParams(vmem_limit_bytes=int(mib * MIB))


def whole(shape):
    return pl.BlockSpec(shape, lambda *_: (0,) * len(shape))


def exact_dot(a, b, ca, cb):
    return lax.dot_general(
        a, b, (((ca,), (cb,)), ((), ())), precision=EXACT, preferred_element_type=jnp.float32
    )


def split(x, terms):
    out = []
    for _ in range(terms):
        out.append(x.astype(jnp.bfloat16))
        x = x - out[-1].astype(jnp.float32)
    return out


def split_dot(a, b, ca, cb):
    total = None
    for order in reversed(range(len(a))):
        for i in range(order + 1):
            part = lax.dot_general(
                a[i], b[order - i], (((ca,), (cb,)), ((), ())), preferred_element_type=jnp.float32
            )
            total = part if total is None else total + part
    return total


def eliminate(block, out_ref):
    n = block.shape[0]
    shape = (PIVOTS, n)
    lane = lax.broadcasted_iota(jnp.int32, shape, 1)
    sub = lax.broadcasted_iota(jnp.int32, shape, 0)
    steps = n // PIVOTS

    def spread(x, k):
        return jnp.broadcast_to(x[:, k : k + 1], shape)

    def row_of(x, i):
        return jnp.broadcast_to(x[i : i + 1, :], shape)

    t = [block[PIVOTS * h : PIVOTS * (h + 1), :] for h in range(steps)]
    pivots = [spread(t[0], j) for j in range(PIVOTS)]
    for g in range(steps):
        k0 = g * PIVOTS
        more = g + 1 < steps
        inside = (lane >= k0) & (lane < k0 + PIVOTS)
        e = [[row_of(pivots[j], i) for j in range(i + 1)] for i in range(PIVOTS)]
        r = [
            jnp.where(inside, jnp.where(lane == k0 + k, 1.0, 0.0), row_of(t[g], k))
            for k in range(PIVOTS)
        ]
        if more:
            c = [spread(t[g + 1], k0 + j) for j in range(PIVOTS)]
            following = [spread(t[g + 1], k0 + PIVOTS + j) for j in range(PIVOTS)]
            rows = jnp.where(inside, 0.0, t[g + 1])
        inv = []
        low = [[None] * PIVOTS for _ in range(PIVOTS)]
        for k in range(PIVOTS):
            inv.append(1.0 / e[k][k])
            for i in range(k + 1, PIVOTS):
                low[i][k] = e[i][k] * inv[k]
                for j in range(k + 1, i + 1):
                    e[i][j] = e[i][j] - low[i][k] * e[j][k]
                r[i] = r[i] - low[i][k] * r[k]
            if more:
                f = c[k] * inv[k]
                for j in range(k + 1, PIVOTS):
                    c[j] = c[j] - f * e[j][k]
                rows = rows - f * r[k]
                for j in range(PIVOTS):
                    following[j] = following[j] - f * row_of(c[k], j)
        done = jnp.zeros(shape, jnp.float32)
        for k in range(PIVOTS):
            done = jnp.where(sub == k, r[k] * lax.rsqrt(e[k][k]), done)
        out_ref[k0 : k0 + PIVOTS, :] = jnp.where(lane < k0 + PIVOTS, done, 0.0)
        if not more:
            break
        t[g + 1] = rows
        pivots = following
        if g + 2 < steps:
            q = [r[k] * inv[k] for k in range(PIVOTS)]
            for k in range(PIVOTS - 1, 0, -1):
                for j in range(k):
                    q[j] = q[j] - low[k][j] * q[k]
            for h in range(g + 2, steps):
                acc = jnp.where(inside, 0.0, t[h])
                for j in range(PIVOTS):
                    acc = acc - spread(t[h], k0 + j) * q[j]
                t[h] = acc


def factor_kernel(d_ref, w_ref, w11_ref, w22_ref):
    m = d_ref.shape[0]
    eliminate(d_ref[:, :m], w11_ref)
    w11 = w11_ref[...]
    l21 = exact_dot(d_ref[:, m : 2 * m], w11, 1, 1)
    rest = d_ref[:, 2 * m :] - exact_dot(l21, l21, 1, 1)
    below = exact_dot(l21, w11, 1, 0)
    eliminate(rest, w22_ref)
    w22 = w22_ref[...]
    w_ref[:, :m] = w11
    w_ref[:, m : 2 * m] = -exact_dot(w22, below, 1, 0)
    w_ref[:, 2 * m :] = w22


def factor_inverse(blocks):
    m = blocks.shape[0]
    return pl.pallas_call(
        factor_kernel,
        out_shape=jax.ShapeDtypeStruct(blocks.shape, jnp.float32),
        scratch_shapes=[pltpu.VMEM((m, m), jnp.float32)] * 2,
        compiler_params=grant(4),
        cost_estimate=pl.CostEstimate(flops=1 << 32, bytes_accessed=1 << 19, transcendentals=0),
    )(blocks)


def full_inverse(w_ref, out_ref):
    m = w_ref.shape[0]
    out_ref[:m, :m] = w_ref[:, :m]
    out_ref[:m, m:] = jnp.zeros((m, m), jnp.float32)
    out_ref[m:, :] = w_ref[:, m:]


def lead_kernel(cov_ref, out_ref, sem):
    copies = []
    for i, (r, c) in enumerate(((0, 0), (1, 0), (1, 1))):
        source = cov_ref.at[pl.ds(r * HALF, HALF), pl.ds(c * HALF, HALF)]
        copies.append(pltpu.make_async_copy(source, out_ref.at[:, pl.ds(i * HALF, HALF)], sem.at[i]))
    for copy in copies:
        copy.start()
    for copy in copies:
        copy.wait()


def lead_blocks(covariance):
    return pl.pallas_call(
        lead_kernel,
        in_specs=[IN_PLACE],
        out_shape=jax.ShapeDtypeStruct((HALF, 3 * HALF), jnp.float32),
        scratch_shapes=[pltpu.SemaphoreType.DMA((3,))],
        compiler_params=grant(63),
        cost_estimate=pl.CostEstimate(flops=0, bytes_accessed=1 << 19, transcendentals=0),
    )(covariance)


def payload_kernel(ratio, cov_ref, pheno_ref, *refs):
    out_refs, (rows_ref, head_ref, sem) = refs[:ratio], refs[ratio:]
    piece = out_refs[0].shape[1]
    copies = [
        pltpu.make_async_copy(pheno_ref.at[pl.ds(0, PANEL), :], head_ref, sem.at[0]),
        pltpu.make_async_copy(cov_ref.at[:, pl.ds(0, PANEL)], rows_ref, sem.at[1]),
    ]
    for m in range(ratio):
        source = cov_ref.at[pl.ds(0, PANEL), pl.ds(m * piece, piece)]
        copies.append(pltpu.make_async_copy(source, out_refs[m].at[pl.ds(0, PANEL), :], sem.at[2 + m]))
    for copy in copies:
        copy.start()
    copies[0].wait()
    traits = head_ref.shape[1]
    height = out_refs[0].shape[0] - PANEL
    at = 0
    for m in range(ratio):
        for i in range(piece // traits):
            out_refs[m][PANEL:, i * traits : (i + 1) * traits] = head_ref[at : at + height, :]
            at += height
    for copy in copies[1:]:
        copy.wait()


def payloads(covariance, phenotypes, ratio):
    n, width = covariance.shape
    traits = phenotypes.shape[1]
    piece = width // ratio
    height = PANEL // ratio // (piece // traits)
    out = jax.ShapeDtypeStruct((PANEL + height, piece), jnp.float32)
    return pl.pallas_call(
        lambda *refs: payload_kernel(ratio, *refs),
        in_specs=[IN_PLACE] * 2,
        out_shape=[out] * ratio + [jax.ShapeDtypeStruct((n, PANEL), jnp.float32)],
        scratch_shapes=[pltpu.VMEM((PANEL, traits), jnp.float32), pltpu.SemaphoreType.DMA((2 + ratio,))],
        compiler_params=grant(61.75),
        cost_estimate=pl.CostEstimate(flops=0, bytes_accessed=4 * MIB, transcendentals=0),
    )(covariance, phenotypes)


def rows_kernel(index_of, *refs):
    options, slab_ref, out_ref, sem = refs[:-3], refs[-3], refs[-2], refs[-1]
    index = index_of(lax.axis_index("row"), lax.axis_index("col"))
    for i, option in enumerate(options):

        @pl.when(index == i)
        def _(option=option):
            copy = pltpu.make_async_copy(option, out_ref, sem)
            copy.start()
            copy.wait()

    @pl.when(index == len(options))
    def _():
        for h in range(0, slab_ref.shape[1], HALF):
            out_ref[h : h + HALF, :] = slab_ref[:, h : h + HALF].T


def pick_rows(index_of, options, slab):
    shape = options[0].shape
    return pl.pallas_call(
        lambda *refs: rows_kernel(index_of, *refs),
        grid=(1,),
        in_specs=[ANYWHERE] * len(options) + [pl.BlockSpec((PANEL, slab.shape[1]), lambda *_: (0, 0))],
        out_specs=whole(shape),
        out_shape=jax.ShapeDtypeStruct(shape, jnp.float32),
        scratch_shapes=[pltpu.SemaphoreType.DMA(())],
        compiler_params=grant(6),
        cost_estimate=pl.CostEstimate(flops=0, bytes_accessed=2 * MIB, transcendentals=0),
    )(*options, slab)


def partner(c, s, col_size):
    return c ^ s if col_size & (col_size - 1) == 0 else lax.rem(c + s, col_size)


def from_partner(p, c, col_size):
    return c ^ p if col_size & (col_size - 1) == 0 else lax.rem(c - p + col_size, col_size)


def solve_kernel(col_size, ratio, *refs):
    w_ref, rows_ref, pheno_ref = refs[:3]
    lead_refs = refs[3 : 3 + ratio]
    panel_ref = refs[3 + ratio]
    part_refs = refs[4 + ratio : 4 + ratio + col_size]
    inv_ref, head_ref, left_ref = refs[4 + ratio + col_size :]
    row, col = lax.axis_index("row"), lax.axis_index("col")
    member = lax.rem(row, ratio)
    head_share = PANEL // ratio
    traits = head_ref.shape[1]
    for s in range(ratio):
        first = lax.rem(member - s + ratio, ratio) * head_share
        height, width = lead_refs[s].shape
        for i in range(width // traits):
            at = pl.multiple_of(first + i * height, 8)
            head_ref[pl.ds(at, height), :] = lead_refs[s][:, i * traits : (i + 1) * traits]
    full_inverse(w_ref, inv_ref)
    inverse = split(inv_ref[...], 3)
    head = split_dot(inverse, split(head_ref[...], 3), 1, 0)
    panel = split_dot(split(rows_ref[...], 3), inverse, 1, 1)
    panel_ref[...] = panel
    left_ref[...] = pheno_ref[...] - split_dot(split(panel, 2), split(head, 2), 1, 0)

    @pl.when(row == 0)
    def _():
        left_ref[:PANEL, :] = head

    share = left_ref.shape[0] // col_size
    for s in range(col_size):
        at = pl.multiple_of(partner(col, s, col_size) * share, share)
        part_refs[s][...] = left_ref[pl.ds(at, share), :]


def solve_rows(blocks, rows, pheno, slabs, col_size):
    n, traits = pheno.shape
    ratio = len(slabs)
    height = slabs[0].shape[0] - PANEL
    part = jax.ShapeDtypeStruct((n // col_size, traits), jnp.float32)
    lead = pl.BlockSpec((height, slabs[0].shape[1]), lambda *_: (PANEL // height, 0))
    outs = [jax.ShapeDtypeStruct(rows.shape, jnp.float32)] + [part] * col_size
    return pl.pallas_call(
        lambda *refs: solve_kernel(col_size, ratio, *refs),
        grid=(1,),
        in_specs=[whole(blocks.shape), whole(rows.shape), whole(pheno.shape)] + [lead] * ratio,
        out_specs=[whole(o.shape) for o in outs],
        out_shape=outs,
        scratch_shapes=[
            pltpu.VMEM((PANEL, PANEL), jnp.float32),
            pltpu.VMEM((PANEL, traits), jnp.float32),
            pltpu.VMEM(pheno.shape, jnp.float32),
        ],
        compiler_params=grant(12),
        cost_estimate=pl.CostEstimate(flops=1 << 30, bytes_accessed=1 << 21, transcendentals=0),
    )(blocks, rows, pheno, *slabs)


def trailing_kernel(ratio, *refs):
    w_ref, panel_ref, cov_ref = refs[:3]
    slab_refs = refs[3 : 3 + ratio]
    out_ref, inv_ref, high_ref, low_ref = refs[3 + ratio :]
    row, col = lax.axis_index("row"), lax.axis_index("col")
    member = lax.rem(row, ratio)
    step = pl.program_id(0)

    @pl.when(step == 0)
    def _():
        full_inverse(w_ref, inv_ref)
        inverse = split(inv_ref[...], 3)
        for s in range(ratio):
            piece = slab_refs[s].shape[1]
            first = lax.rem(member - s + ratio, ratio) * piece
            for h in range(0, piece, PANEL):
                right = split_dot(inverse, split(slab_refs[s][:, h : h + PANEL], 3), 1, 0)
                at = pl.ds(pl.multiple_of(first + h, PANEL), PANEL)
                high_ref[:, at], low_ref[:, at] = split(right, 2)

    panel = panel_ref[...]
    lead = (row == 0) & (step * panel.shape[0] < PANEL)
    below = jnp.where(lead, 0.0, panel)
    right = [high_ref[...], low_ref[...]]
    out_ref[...] = cov_ref[...] - split_dot(split(below, 2), right, 1, 0)

    @pl.when(col == 0)
    def _():
        out_ref[:, :PANEL] = panel


def trailing_update(blocks, panel, covariance, slabs):
    n, width = covariance.shape
    ratio = len(slabs)
    tall = min(n, PANEL)
    slab = pl.BlockSpec((PANEL, slabs[0].shape[1]), lambda i: (0, 0))
    return pl.pallas_call(
        lambda *refs: trailing_kernel(ratio, *refs),
        grid=(n // tall,),
        in_specs=[
            whole(blocks.shape),
            pl.BlockSpec((tall, PANEL), lambda i: (i, 0)),
            pl.BlockSpec((tall, width), lambda i: (i, 0)),
        ]
        + [slab] * ratio,
        out_specs=pl.BlockSpec((tall, width), lambda i: (i, 0)),
        out_shape=jax.ShapeDtypeStruct(covariance.shape, jnp.float32),
        scratch_shapes=[
            pltpu.VMEM((PANEL, PANEL), jnp.float32),
            pltpu.VMEM((PANEL, width), jnp.bfloat16),
            pltpu.VMEM((PANEL, width), jnp.bfloat16),
        ],
        compiler_params=grant(16),
        cost_estimate=pl.CostEstimate(flops=1 << 31, bytes_accessed=6 << 20, transcendentals=0),
    )(blocks, panel, covariance, *slabs)


def tree(nodes, level, levels, edges):
    if len(nodes) < 2:
        return
    half = len(nodes) // 2
    edges.append((level, levels[nodes[0]], nodes[0], nodes[half]))
    levels[nodes[half]] = level
    tree(nodes[:half], level + 1, levels, edges)
    tree(nodes[half:], level + 1, levels, edges)


def bit_reversed(count):
    bits = max(count - 1, 0).bit_length()
    order = [int(format(i, "0%db" % bits)[::-1], 2) if bits else 0 for i in range(1 << bits)]
    return [i for i in order if i < count]


def choose(index, options):
    out = options[0]
    for i in range(1, len(options)):
        out = jnp.where(index == i, options[i], out)
    return out


def look_up(table, at):
    out = table[0]
    for i, value in enumerate(table):
        if value != table[0]:
            out = jnp.where(at == i, value, out)
    return out


def shards(covariance, phenotypes):
    row_size, col_size = lax.axis_size("row"), lax.axis_size("col")
    row_index, col_index = lax.axis_index("row"), lax.axis_index("col")
    ratio = row_size // col_size
    groups = row_size // ratio
    group, member = row_index // ratio, lax.rem(row_index, ratio)

    def place(r, c):
        return r * col_size + c

    def send(x, pairs):
        return lax.ppermute(x, AXES, [(place(*a), place(*b)) for a, b in pairs])

    every_group = [(k, c) for k in range(groups) for c in range(col_size)]

    blocks = lead_blocks(covariance)
    found = []
    tree(list(range(col_size)), 1, {0: 0}, found)
    steps = {}
    for lv, sl, s, d in found:
        steps.setdefault(lv, []).append((s, d))
    diag = blocks
    for lv in sorted(steps):
        got = send(diag, [((0, s), (0, d)) for s, d in steps[lv]])
        new = [int(c in [d for _, d in steps[lv]]) for c in range(col_size)]
        diag = jnp.where(look_up(new, col_index) > 0, got, diag)

    *pieces, own_rows = payloads(covariance, phenotypes, ratio)
    start = [pieces[0]]
    for m in range(1, ratio):
        start.append(send(pieces[m], [((0, c), (m, c)) for c in range(col_size)]))
    start = choose(row_index, start)
    stages = {}
    came = {}
    for m in range(ratio):
        nodes = list(range(groups)) if m % 2 == 0 else bit_reversed(groups)
        found = []
        tree(nodes, 1, {0: 0}, found)
        for lv, sl, a, b in found:
            stages.setdefault((lv, sl), []).append((a * ratio + m, b * ratio + m))
            came[b * ratio + m] = (lv, sl)
    keys = sorted(stages)
    results = [start]
    held = {0: start}
    for key in keys:
        pairs = [((a, c), (b, c)) for a, b in stages[key] for c in range(col_size)]
        got = send(held[key[1]], pairs)
        results.append(got)
        if key[0] in held:
            here = [int(came.get(r) == key) for r in range(row_size)]
            held[key[0]] = jnp.where(look_up(here, row_index) > 0, got, held[key[0]])
        else:
            held[key[0]] = got
    source = look_up([keys.index(came[r]) + 1 if r in came else 0 for r in range(row_size)], row_index)

    relay_from = col_size // 2
    targets = []
    for r in range(row_size):
        k = r // ratio
        if k:
            line = [c for c in range(1, col_size) if c != k]
        else:
            line = [relay_from] + [c for c in range(1, col_size - 1) if c != relay_from]
        targets.append(line)
    arrived = []
    for j in range(col_size - 2):
        arrived.append(send(own_rows, [((r, 0), (r, targets[r][j])) for r in range(row_size) if j < len(targets[r])]))

    inverse = factor_inverse(diag)
    got = [inverse]
    for k in range(1, groups):
        got.append(send(inverse, [((0, c), (k * ratio, c)) for c in range(col_size)]))
    inverse = choose(group, got)

    arrived.append(send(arrived[0], [((r, relay_from), (r, col_size - 1)) for r in range(ratio)]))
    mine = choose(source, results)
    slabs = [mine]
    for s in range(1, ratio):
        slabs.append(
            send(
                mine,
                [((k * ratio + m, c), (k * ratio + (m + s) % ratio, c)) for k, c in every_group for m in range(ratio)],
            )
        )

    def index_of(row, col):
        k = row // ratio
        first = jnp.where(
            col == relay_from,
            1,
            jnp.where(col == col_size - 1, col_size - 1, jnp.where(col < relay_from, col + 1, col)),
        )
        later = jnp.where(col == k, col_size, jnp.where(col < k, col, col - 1))
        return jnp.where(col == 0, 0, jnp.where(k == 0, first, later))

    panel_raw = pick_rows(index_of, [own_rows] + arrived, mine)

    got = [inverse]
    for m in range(1, ratio):
        got.append(send(inverse, [((k * ratio, c), (k * ratio + m, c)) for k, c in every_group]))
    inverse = choose(member, got)

    panel, *parts = solve_rows(inverse, panel_raw, phenotypes, slabs, col_size)
    gathered = [parts[0]]
    for s in range(1, col_size):
        pairs = [((r, c), (r, int(partner(c, s, col_size)))) for r in range(row_size) for c in range(col_size)]
        gathered.append(send(parts[s], pairs))
    updated = trailing_update(inverse, panel, covariance, slabs)
    solved = jnp.concatenate(
        [choose(from_partner(p, col_index, col_size), gathered) for p in range(col_size)], axis=1
    )
    return (updated, solved)


def solution(mesh):
    placed = (P("row", "col"), P("row", "col"))

    return jax.shard_map(
        shards,
        mesh=mesh,
        in_specs=placed,
        out_specs=(P("row", "col"), P(("row", "col"), None)),
        check_vma=False,
    )
```

```python
import jax
import jax.numpy as jnp
from jax import lax
from jax.experimental import pallas as pl
from jax.experimental.pallas import tpu as pltpu
from jax.sharding import PartitionSpec as P


PANEL = 256
HALF = PANEL // 2
PIVOTS = 8
EXACT = lax.Precision.HIGHEST
AXES = ("row", "col")


MIB = 1 << 20
ANYWHERE = pl.BlockSpec(memory_space=pl.ANY)
IN_PLACE = pl.BlockSpec(memory_space=pltpu.HBM)


def grant(mib):
    return pltpu.CompilerParams(vmem_limit_bytes=int(mib * MIB))


def whole(shape):
    return pl.BlockSpec(shape, lambda *_: (0,) * len(shape))


def exact_dot(a, b, ca, cb):
    return lax.dot_general(
        a, b, (((ca,), (cb,)), ((), ())), precision=EXACT, preferred_element_type=jnp.float32
    )


def split(x, terms):
    out = []
    for _ in range(terms):
        out.append(x.astype(jnp.bfloat16))
        x = x - out[-1].astype(jnp.float32)
    return out


def split_dot(a, b, ca, cb):
    total = None
    for order in reversed(range(len(a))):
        for i in range(order + 1):
            part = lax.dot_general(
                a[i], b[order - i], (((ca,), (cb,)), ((), ())), preferred_element_type=jnp.float32
            )
            total = part if total is None else total + part
    return total


def eliminate(block, out_ref):
    n = block.shape[0]
    shape = (PIVOTS, n)
    lane = lax.broadcasted_iota(jnp.int32, shape, 1)
    sub = lax.broadcasted_iota(jnp.int32, shape, 0)
    steps = n // PIVOTS

    def spread(x, k):
        return jnp.broadcast_to(x[:, k : k + 1], shape)

    def row_of(x, i):
        return jnp.broadcast_to(x[i : i + 1, :], shape)

    t = [block[PIVOTS * h : PIVOTS * (h + 1), :] for h in range(steps)]
    pivots = [spread(t[0], j) for j in range(PIVOTS)]
    for g in range(steps):
        k0 = g * PIVOTS
        more = g + 1 < steps
        inside = (lane >= k0) & (lane < k0 + PIVOTS)
        e = [[row_of(pivots[j], i) for j in range(i + 1)] for i in range(PIVOTS)]
        r = [
            jnp.where(inside, jnp.where(lane == k0 + k, 1.0, 0.0), row_of(t[g], k))
            for k in range(PIVOTS)
        ]
        if more:
            c = [spread(t[g + 1], k0 + j) for j in range(PIVOTS)]
            following = [spread(t[g + 1], k0 + PIVOTS + j) for j in range(PIVOTS)]
            rows = jnp.where(inside, 0.0, t[g + 1])
        inv = []
        low = [[None] * PIVOTS for _ in range(PIVOTS)]
        for k in range(PIVOTS):
            inv.append(1.0 / e[k][k])
            for i in range(k + 1, PIVOTS):
                low[i][k] = e[i][k] * inv[k]
                for j in range(k + 1, i + 1):
                    e[i][j] = e[i][j] - low[i][k] * e[j][k]
                r[i] = r[i] - low[i][k] * r[k]
            if more:
                f = c[k] * inv[k]
                for j in range(k + 1, PIVOTS):
                    c[j] = c[j] - f * e[j][k]
                rows = rows - f * r[k]
                for j in range(PIVOTS):
                    following[j] = following[j] - f * row_of(c[k], j)
        done = jnp.zeros(shape, jnp.float32)
        for k in range(PIVOTS):
            done = jnp.where(sub == k, r[k] * lax.rsqrt(e[k][k]), done)
        out_ref[k0 : k0 + PIVOTS, :] = jnp.where(lane < k0 + PIVOTS, done, 0.0)
        if not more:
            break
        t[g + 1] = rows
        pivots = following
        if g + 2 < steps:
            q = [r[k] * inv[k] for k in range(PIVOTS)]
            for k in range(PIVOTS - 1, 0, -1):
                for j in range(k):
                    q[j] = q[j] - low[k][j] * q[k]
            for h in range(g + 2, steps):
                acc = jnp.where(inside, 0.0, t[h])
                for j in range(PIVOTS):
                    acc = acc - spread(t[h], k0 + j) * q[j]
                t[h] = acc


def factor_kernel(d_ref, w_ref, w11_ref, w22_ref):
    m = d_ref.shape[0]
    eliminate(d_ref[:, :m], w11_ref)
    w11 = w11_ref[...]
    l21 = exact_dot(d_ref[:, m : 2 * m], w11, 1, 1)
    rest = d_ref[:, 2 * m :] - exact_dot(l21, l21, 1, 1)
    below = exact_dot(l21, w11, 1, 0)
    eliminate(rest, w22_ref)
    w22 = w22_ref[...]
    w_ref[:, :m] = w11
    w_ref[:, m : 2 * m] = -exact_dot(w22, below, 1, 0)
    w_ref[:, 2 * m :] = w22


def factor_inverse(blocks):
    m = blocks.shape[0]
    return pl.pallas_call(
        factor_kernel,
        out_shape=jax.ShapeDtypeStruct(blocks.shape, jnp.float32),
        scratch_shapes=[pltpu.VMEM((m, m), jnp.float32)] * 2,
        compiler_params=grant(4),
        cost_estimate=pl.CostEstimate(flops=1 << 32, bytes_accessed=1 << 19, transcendentals=0),
    )(blocks)


def full_inverse(w_ref, out_ref):
    m = w_ref.shape[0]
    out_ref[:m, :m] = w_ref[:, :m]
    out_ref[:m, m:] = jnp.zeros((m, m), jnp.float32)
    out_ref[m:, :] = w_ref[:, m:]


def cut_kernel(ratio, cov_ref, pheno_ref, lead_ref, *refs):
    out_refs, (rows_ref, head_ref, sem) = refs[:ratio], refs[ratio:]
    piece = out_refs[0].shape[1]
    copies = [
        pltpu.make_async_copy(pheno_ref.at[pl.ds(0, PANEL), :], head_ref, sem.at[0]),
        pltpu.make_async_copy(cov_ref.at[:, pl.ds(0, PANEL)], rows_ref, sem.at[1]),
    ]
    for m in range(ratio):
        source = cov_ref.at[pl.ds(0, PANEL), pl.ds(m * piece, piece)]
        copies.append(pltpu.make_async_copy(source, out_refs[m].at[pl.ds(0, PANEL), :], sem.at[2 + m]))
    for i, (r, c) in enumerate(((0, 0), (1, 0), (1, 1))):
        source = cov_ref.at[pl.ds(r * HALF, HALF), pl.ds(c * HALF, HALF)]
        target = lead_ref.at[:, pl.ds(i * HALF, HALF)]
        copies.append(pltpu.make_async_copy(source, target, sem.at[2 + ratio + i]))
    for copy in copies:
        copy.start()
    copies[0].wait()
    traits = head_ref.shape[1]
    height = out_refs[0].shape[0] - PANEL
    at = 0
    for m in range(ratio):
        for i in range(piece // traits):
            out_refs[m][PANEL:, i * traits : (i + 1) * traits] = head_ref[at : at + height, :]
            at += height
    for copy in copies[1:]:
        copy.wait()


def cut(covariance, phenotypes, ratio):
    n, width = covariance.shape
    traits = phenotypes.shape[1]
    piece = width // ratio
    height = PANEL // ratio // (piece // traits)
    out = jax.ShapeDtypeStruct((PANEL + height, piece), jnp.float32)
    return pl.pallas_call(
        lambda *refs: cut_kernel(ratio, *refs),
        in_specs=[IN_PLACE] * 2,
        out_shape=[jax.ShapeDtypeStruct((HALF, 3 * HALF), jnp.float32)]
        + [out] * ratio
        + [jax.ShapeDtypeStruct((n, PANEL), jnp.float32)],
        scratch_shapes=[pltpu.VMEM((PANEL, traits), jnp.float32), pltpu.SemaphoreType.DMA((5 + ratio,))],
        compiler_params=grant(61.9),
        cost_estimate=pl.CostEstimate(flops=0, bytes_accessed=4 * MIB, transcendentals=0),
    )(covariance, phenotypes)


def pick_kernel(index_of, *refs):
    options, out_ref = refs[:-1], refs[-1]
    index = index_of(lax.axis_index("row"))
    for i, option in enumerate(options):

        @pl.when(index == i)
        def _(option=option):
            out_ref[...] = option[...]


def pick(index_of, options):
    shape = options[0].shape
    return pl.pallas_call(
        lambda *refs: pick_kernel(index_of, *refs),
        in_specs=[pl.BlockSpec(memory_space=pltpu.VMEM)] * len(options),
        out_specs=pl.BlockSpec(memory_space=pltpu.VMEM),
        out_shape=jax.ShapeDtypeStruct(shape, jnp.float32),
        compiler_params=grant(1 + (len(options) + 1) * options[0].size * 4 / MIB),
        cost_estimate=pl.CostEstimate(flops=0, bytes_accessed=1 << 19, transcendentals=0),
    )(*options)


def rows_kernel(index_of, *refs):
    options, slab_ref, out_ref, sem = refs[:-3], refs[-3], refs[-2], refs[-1]
    index = index_of(lax.axis_index("row"), lax.axis_index("col"))
    for i, option in enumerate(options):

        @pl.when(index == i)
        def _(option=option):
            copy = pltpu.make_async_copy(option, out_ref, sem)
            copy.start()
            copy.wait()

    @pl.when(index == len(options))
    def _():
        for h in range(0, slab_ref.shape[1], HALF):
            out_ref[h : h + HALF, :] = slab_ref[:, h : h + HALF].T


def pick_rows(index_of, options, slab):
    shape = options[0].shape
    return pl.pallas_call(
        lambda *refs: rows_kernel(index_of, *refs),
        grid=(1,),
        in_specs=[ANYWHERE] * len(options) + [pl.BlockSpec((PANEL, slab.shape[1]), lambda *_: (0, 0))],
        out_specs=whole(shape),
        out_shape=jax.ShapeDtypeStruct(shape, jnp.float32),
        scratch_shapes=[pltpu.SemaphoreType.DMA(())],
        compiler_params=grant(6),
        cost_estimate=pl.CostEstimate(flops=0, bytes_accessed=2 * MIB, transcendentals=0),
    )(*options, slab)


def partner(c, s, col_size):
    return c ^ s if col_size & (col_size - 1) == 0 else lax.rem(c + s, col_size)


def from_partner(p, c, col_size):
    return c ^ p if col_size & (col_size - 1) == 0 else lax.rem(c - p + col_size, col_size)


def solve_kernel(col_size, ratio, *refs):
    w_ref, rows_ref, pheno_ref = refs[:3]
    lead_refs = refs[3 : 3 + ratio]
    panel_ref = refs[3 + ratio]
    part_refs = refs[4 + ratio : 4 + ratio + col_size]
    inv_ref, head_ref, left_ref = refs[4 + ratio + col_size :]
    row, col = lax.axis_index("row"), lax.axis_index("col")
    member = lax.rem(row, ratio)
    head_share = PANEL // ratio
    traits = head_ref.shape[1]
    for s in range(ratio):
        first = lax.rem(member - s + ratio, ratio) * head_share
        height, width = lead_refs[s].shape
        for i in range(width // traits):
            at = pl.multiple_of(first + i * height, 8)
            head_ref[pl.ds(at, height), :] = lead_refs[s][:, i * traits : (i + 1) * traits]
    full_inverse(w_ref, inv_ref)
    inverse = split(inv_ref[...], 3)
    head = split_dot(inverse, split(head_ref[...], 3), 1, 0)
    panel = split_dot(split(rows_ref[...], 3), inverse, 1, 1)
    panel_ref[...] = panel
    left_ref[...] = pheno_ref[...] - split_dot(split(panel, 2), split(head, 2), 1, 0)

    @pl.when(row == 0)
    def _():
        left_ref[:PANEL, :] = head

    share = left_ref.shape[0] // col_size
    for s in range(col_size):
        at = pl.multiple_of(partner(col, s, col_size) * share, share)
        part_refs[s][...] = left_ref[pl.ds(at, share), :]


def solve_rows(blocks, rows, pheno, slabs, col_size):
    n, traits = pheno.shape
    ratio = len(slabs)
    height = slabs[0].shape[0] - PANEL
    part = jax.ShapeDtypeStruct((n // col_size, traits), jnp.float32)
    lead = pl.BlockSpec((height, slabs[0].shape[1]), lambda *_: (PANEL // height, 0))
    outs = [jax.ShapeDtypeStruct(rows.shape, jnp.float32)] + [part] * col_size
    return pl.pallas_call(
        lambda *refs: solve_kernel(col_size, ratio, *refs),
        grid=(1,),
        in_specs=[whole(blocks.shape), whole(rows.shape), whole(pheno.shape)] + [lead] * ratio,
        out_specs=[whole(o.shape) for o in outs],
        out_shape=outs,
        scratch_shapes=[
            pltpu.VMEM((PANEL, PANEL), jnp.float32),
            pltpu.VMEM((PANEL, traits), jnp.float32),
            pltpu.VMEM(pheno.shape, jnp.float32),
        ],
        compiler_params=grant(12),
        cost_estimate=pl.CostEstimate(flops=1 << 30, bytes_accessed=1 << 21, transcendentals=0),
    )(blocks, rows, pheno, *slabs)


def trailing_kernel(ratio, *refs):
    w_ref, panel_ref, cov_ref = refs[:3]
    slab_refs = refs[3 : 3 + ratio]
    out_ref, inv_ref, high_ref, low_ref = refs[3 + ratio :]
    row, col = lax.axis_index("row"), lax.axis_index("col")
    member = lax.rem(row, ratio)
    step = pl.program_id(0)

    @pl.when(step == 0)
    def _():
        full_inverse(w_ref, inv_ref)
        inverse = split(inv_ref[...], 3)
        for s in range(ratio):
            piece = slab_refs[s].shape[1]
            first = lax.rem(member - s + ratio, ratio) * piece
            for h in range(0, piece, PANEL):
                right = split_dot(inverse, split(slab_refs[s][:, h : h + PANEL], 3), 1, 0)
                at = pl.ds(pl.multiple_of(first + h, PANEL), PANEL)
                high_ref[:, at], low_ref[:, at] = split(right, 2)

    panel = panel_ref[...]
    lead = (row == 0) & (step * panel.shape[0] < PANEL)
    below = jnp.where(lead, 0.0, panel)
    right = [high_ref[...], low_ref[...]]
    out_ref[...] = cov_ref[...] - split_dot(split(below, 2), right, 1, 0)

    @pl.when(col == 0)
    def _():
        out_ref[:, :PANEL] = panel


def trailing_update(blocks, panel, covariance, slabs):
    n, width = covariance.shape
    ratio = len(slabs)
    tall = min(n, PANEL)
    slab = pl.BlockSpec((PANEL, slabs[0].shape[1]), lambda i: (0, 0))
    return pl.pallas_call(
        lambda *refs: trailing_kernel(ratio, *refs),
        grid=(n // tall,),
        in_specs=[
            whole(blocks.shape),
            pl.BlockSpec((tall, PANEL), lambda i: (i, 0)),
            pl.BlockSpec((tall, width), lambda i: (i, 0)),
        ]
        + [slab] * ratio,
        out_specs=pl.BlockSpec((tall, width), lambda i: (i, 0)),
        out_shape=jax.ShapeDtypeStruct(covariance.shape, jnp.float32),
        scratch_shapes=[
            pltpu.VMEM((PANEL, PANEL), jnp.float32),
            pltpu.VMEM((PANEL, width), jnp.bfloat16),
            pltpu.VMEM((PANEL, width), jnp.bfloat16),
        ],
        compiler_params=grant(16),
        cost_estimate=pl.CostEstimate(flops=1 << 31, bytes_accessed=6 << 20, transcendentals=0),
    )(blocks, panel, covariance, *slabs)


def tree(nodes, level, levels, edges):
    if len(nodes) < 2:
        return
    half = len(nodes) // 2
    edges.append((level, levels[nodes[0]], nodes[0], nodes[half]))
    levels[nodes[half]] = level
    tree(nodes[:half], level + 1, levels, edges)
    tree(nodes[half:], level + 1, levels, edges)


def bit_reversed(count):
    bits = max(count - 1, 0).bit_length()
    order = [int(format(i, "0%db" % bits)[::-1], 2) if bits else 0 for i in range(1 << bits)]
    return [i for i in order if i < count]


def choose(index, options):
    out = options[0]
    for i in range(1, len(options)):
        out = jnp.where(index == i, options[i], out)
    return out


def look_up(table, at):
    out = table[0]
    for i, value in enumerate(table):
        if value != table[0]:
            out = jnp.where(at == i, value, out)
    return out


def shards(covariance, phenotypes):
    row_size, col_size = lax.axis_size("row"), lax.axis_size("col")
    row_index, col_index = lax.axis_index("row"), lax.axis_index("col")
    ratio = row_size // col_size
    groups = row_size // ratio
    member = lax.rem(row_index, ratio)

    def place(r, c):
        return r * col_size + c

    def send(x, pairs):
        return lax.ppermute(x, AXES, [(place(*a), place(*b)) for a, b in pairs])

    every_group = [(k, c) for k in range(groups) for c in range(col_size)]

    blocks, *pieces, own_rows = cut(covariance, phenotypes, ratio)
    found = []
    tree(list(range(col_size)), 1, {0: 0}, found)
    steps = {}
    for lv, sl, s, d in found:
        steps.setdefault(lv, []).append((s, d))
    diag = blocks
    for lv in sorted(steps):
        got = send(diag, [((0, s), (0, d)) for s, d in steps[lv]])
        new = [int(c in [d for _, d in steps[lv]]) for c in range(col_size)]
        diag = jnp.where(look_up(new, col_index) > 0, got, diag)

    start = [pieces[0]]
    for m in range(1, ratio):
        start.append(send(pieces[m], [((0, c), (m, c)) for c in range(col_size)]))
    start = choose(row_index, start)
    stages = {}
    came = {}
    for m in range(ratio):
        nodes = list(range(groups)) if m % 2 == 0 else bit_reversed(groups)
        found = []
        tree(nodes, 1, {0: 0}, found)
        for lv, sl, a, b in found:
            stages.setdefault((lv, sl), []).append((a * ratio + m, b * ratio + m))
            came[b * ratio + m] = (lv, sl)
    keys = sorted(stages)
    results = [start]
    held = {0: start}
    for key in keys:
        pairs = [((a, c), (b, c)) for a, b in stages[key] for c in range(col_size)]
        got = send(held[key[1]], pairs)
        results.append(got)
        if key[0] in held:
            here = [int(came.get(r) == key) for r in range(row_size)]
            held[key[0]] = jnp.where(look_up(here, row_index) > 0, got, held[key[0]])
        else:
            held[key[0]] = got
    source = look_up([keys.index(came[r]) + 1 if r in came else 0 for r in range(row_size)], row_index)

    relay_from = col_size // 2
    targets = []
    for r in range(row_size):
        k = r // ratio
        if k:
            line = [c for c in range(1, col_size) if c != k]
        else:
            line = [relay_from] + [c for c in range(1, col_size - 1) if c != relay_from]
        targets.append(line)
    arrived = []
    for j in range(col_size - 2):
        arrived.append(send(own_rows, [((r, 0), (r, targets[r][j])) for r in range(row_size) if j < len(targets[r])]))

    inverse = factor_inverse(diag)
    got = [inverse]
    for k in range(1, groups):
        got.append(send(inverse, [((0, c), (k * ratio, c)) for c in range(col_size)]))
    inverse = pick(lambda row: row // ratio, got)

    arrived.append(send(arrived[0], [((r, relay_from), (r, col_size - 1)) for r in range(ratio)]))
    mine = choose(source, results)
    slabs = [mine]
    for s in range(1, ratio):
        slabs.append(
            send(
                mine,
                [((k * ratio + m, c), (k * ratio + (m + s) % ratio, c)) for k, c in every_group for m in range(ratio)],
            )
        )

    def index_of(row, col):
        k = row // ratio
        first = jnp.where(
            col == relay_from,
            1,
            jnp.where(col == col_size - 1, col_size - 1, jnp.where(col < relay_from, col + 1, col)),
        )
        later = jnp.where(col == k, col_size, jnp.where(col < k, col, col - 1))
        return jnp.where(col == 0, 0, jnp.where(k == 0, first, later))

    panel_raw = pick_rows(index_of, [own_rows] + arrived, mine)

    got = [inverse]
    for m in range(1, ratio):
        got.append(send(inverse, [((k * ratio, c), (k * ratio + m, c)) for k, c in every_group]))
    inverse = pick(lambda row: lax.rem(row, ratio), got)

    panel, *parts = solve_rows(inverse, panel_raw, phenotypes, slabs, col_size)
    gathered = [parts[0]]
    for s in range(1, col_size):
        pairs = [((r, c), (r, int(partner(c, s, col_size)))) for r in range(row_size) for c in range(col_size)]
        gathered.append(send(parts[s], pairs))
    updated = trailing_update(inverse, panel, covariance, slabs)
    solved = jnp.concatenate(
        [choose(from_partner(p, col_index, col_size), gathered) for p in range(col_size)], axis=1
    )
    return (updated, solved)


def solution(mesh):
    placed = (P("row", "col"), P("row", "col"))

    return jax.shard_map(
        shards,
        mesh=mesh,
        in_specs=placed,
        out_specs=(P("row", "col"), P(("row", "col"), None)),
        check_vma=False,
    )
```

```python
import jax
import jax.numpy as jnp
from jax import lax
from jax.experimental import pallas as pl
from jax.experimental.pallas import tpu as pltpu
from jax.sharding import PartitionSpec as P


PANEL = 256
HALF = PANEL // 2
PIVOTS = 8
EXACT = lax.Precision.HIGHEST
AXES = ("row", "col")


MIB = 1 << 20
ANYWHERE = pl.BlockSpec(memory_space=pl.ANY)
IN_PLACE = pl.BlockSpec(memory_space=pltpu.HBM)


def grant(mib):
    return pltpu.CompilerParams(vmem_limit_bytes=int(mib * MIB))


def whole(shape):
    return pl.BlockSpec(shape, lambda *_: (0,) * len(shape))


def exact_dot(a, b, ca, cb):
    return lax.dot_general(
        a, b, (((ca,), (cb,)), ((), ())), precision=EXACT, preferred_element_type=jnp.float32
    )


def split(x, terms):
    out = []
    for _ in range(terms):
        out.append(x.astype(jnp.bfloat16))
        x = x - out[-1].astype(jnp.float32)
    return out


def split_dot(a, b, ca, cb):
    total = None
    for order in reversed(range(len(a))):
        for i in range(order + 1):
            part = lax.dot_general(
                a[i], b[order - i], (((ca,), (cb,)), ((), ())), preferred_element_type=jnp.float32
            )
            total = part if total is None else total + part
    return total


def eliminate(block, out_ref):
    n = block.shape[0]
    shape = (PIVOTS, n)
    lane = lax.broadcasted_iota(jnp.int32, shape, 1)
    sub = lax.broadcasted_iota(jnp.int32, shape, 0)
    steps = n // PIVOTS

    def spread(x, k):
        return jnp.broadcast_to(x[:, k : k + 1], shape)

    def row_of(x, i):
        return jnp.broadcast_to(x[i : i + 1, :], shape)

    t = [block[PIVOTS * h : PIVOTS * (h + 1), :] for h in range(steps)]
    pivots = [spread(t[0], j) for j in range(PIVOTS)]
    for g in range(steps):
        k0 = g * PIVOTS
        more = g + 1 < steps
        inside = (lane >= k0) & (lane < k0 + PIVOTS)
        e = [[row_of(pivots[j], i) for j in range(i + 1)] for i in range(PIVOTS)]
        r = [
            jnp.where(inside, jnp.where(lane == k0 + k, 1.0, 0.0), row_of(t[g], k))
            for k in range(PIVOTS)
        ]
        if more:
            c = [spread(t[g + 1], k0 + j) for j in range(PIVOTS)]
            following = [spread(t[g + 1], k0 + PIVOTS + j) for j in range(PIVOTS)]
            rows = jnp.where(inside, 0.0, t[g + 1])
        inv = []
        low = [[None] * PIVOTS for _ in range(PIVOTS)]
        for k in range(PIVOTS):
            inv.append(1.0 / e[k][k])
            for i in range(k + 1, PIVOTS):
                low[i][k] = e[i][k] * inv[k]
                for j in range(k + 1, i + 1):
                    e[i][j] = e[i][j] - low[i][k] * e[j][k]
                r[i] = r[i] - low[i][k] * r[k]
            if more:
                f = c[k] * inv[k]
                for j in range(k + 1, PIVOTS):
                    c[j] = c[j] - f * e[j][k]
                rows = rows - f * r[k]
                for j in range(PIVOTS):
                    following[j] = following[j] - f * row_of(c[k], j)
        done = jnp.zeros(shape, jnp.float32)
        for k in range(PIVOTS):
            done = jnp.where(sub == k, r[k] * lax.rsqrt(e[k][k]), done)
        out_ref[k0 : k0 + PIVOTS, :] = jnp.where(lane < k0 + PIVOTS, done, 0.0)
        if not more:
            break
        t[g + 1] = rows
        pivots = following
        if g + 2 < steps:
            q = [r[k] * inv[k] for k in range(PIVOTS)]
            for k in range(PIVOTS - 1, 0, -1):
                for j in range(k):
                    q[j] = q[j] - low[k][j] * q[k]
            for h in range(g + 2, steps):
                acc = jnp.where(inside, 0.0, t[h])
                for j in range(PIVOTS):
                    acc = acc - spread(t[h], k0 + j) * q[j]
                t[h] = acc


def factor_kernel(*refs):
    options, (w_ref, d_ref, w11_ref, w22_ref, sem) = refs[:-5], refs[-5:]
    fetch(lax.axis_index("col"), options, d_ref, sem)
    m = d_ref.shape[0]
    eliminate(d_ref[:, :m], w11_ref)
    w11 = w11_ref[...]
    l21 = exact_dot(d_ref[:, m : 2 * m], w11, 1, 1)
    rest = d_ref[:, 2 * m :] - exact_dot(l21, l21, 1, 1)
    below = exact_dot(l21, w11, 1, 0)
    eliminate(rest, w22_ref)
    w22 = w22_ref[...]
    w_ref[:, :m] = w11
    w_ref[:, m : 2 * m] = -exact_dot(w22, below, 1, 0)
    w_ref[:, 2 * m :] = w22


def factor_inverse(options):
    shape = options[0].shape
    square = pltpu.VMEM((shape[0], shape[0]), jnp.float32)
    return pl.pallas_call(
        factor_kernel,
        in_specs=[ANYWHERE] * len(options),
        out_shape=jax.ShapeDtypeStruct(shape, jnp.float32),
        scratch_shapes=[pltpu.VMEM(shape, jnp.float32), square, square, pltpu.SemaphoreType.DMA(())],
        compiler_params=grant(4),
        cost_estimate=pl.CostEstimate(flops=1 << 32, bytes_accessed=1 << 19, transcendentals=0),
    )(*options)


def full_inverse(w_ref, out_ref):
    m = w_ref.shape[0]
    out_ref[:m, :m] = w_ref[:, :m]
    out_ref[:m, m:] = jnp.zeros((m, m), jnp.float32)
    out_ref[m:, :] = w_ref[:, m:]


def cut_kernel(ratio, cov_ref, pheno_ref, lead_ref, *refs):
    out_refs, (rows_ref, head_ref, sem) = refs[:ratio], refs[ratio:]
    piece = out_refs[0].shape[1]
    copies = [
        pltpu.make_async_copy(pheno_ref.at[pl.ds(0, PANEL), :], head_ref, sem.at[0]),
        pltpu.make_async_copy(cov_ref.at[:, pl.ds(0, PANEL)], rows_ref, sem.at[1]),
    ]
    for m in range(ratio):
        source = cov_ref.at[pl.ds(0, PANEL), pl.ds(m * piece, piece)]
        copies.append(pltpu.make_async_copy(source, out_refs[m].at[pl.ds(0, PANEL), :], sem.at[2 + m]))
    for i, (r, c) in enumerate(((0, 0), (1, 0), (1, 1))):
        source = cov_ref.at[pl.ds(r * HALF, HALF), pl.ds(c * HALF, HALF)]
        target = lead_ref.at[:, pl.ds(i * HALF, HALF)]
        copies.append(pltpu.make_async_copy(source, target, sem.at[2 + ratio + i]))
    for copy in copies:
        copy.start()
    copies[0].wait()
    traits = head_ref.shape[1]
    height = out_refs[0].shape[0] - PANEL
    at = 0
    for m in range(ratio):
        for i in range(piece // traits):
            out_refs[m][PANEL:, i * traits : (i + 1) * traits] = head_ref[at : at + height, :]
            at += height
    for copy in copies[1:]:
        copy.wait()


def cut(covariance, phenotypes, ratio):
    n, width = covariance.shape
    traits = phenotypes.shape[1]
    piece = width // ratio
    height = PANEL // ratio // (piece // traits)
    out = jax.ShapeDtypeStruct((PANEL + height, piece), jnp.float32)
    return pl.pallas_call(
        lambda *refs: cut_kernel(ratio, *refs),
        in_specs=[IN_PLACE] * 2,
        out_shape=[jax.ShapeDtypeStruct((HALF, 3 * HALF), jnp.float32)]
        + [out] * ratio
        + [jax.ShapeDtypeStruct((n, PANEL), jnp.float32)],
        scratch_shapes=[pltpu.VMEM((PANEL, traits), jnp.float32), pltpu.SemaphoreType.DMA((5 + ratio,))],
        compiler_params=grant(61.9),
        cost_estimate=pl.CostEstimate(flops=0, bytes_accessed=4 * MIB, transcendentals=0),
    )(covariance, phenotypes)


def pick_kernel(index_of, *refs):
    options, out_ref = refs[:-1], refs[-1]
    index = index_of(lax.axis_index("row"))
    for i, option in enumerate(options):

        @pl.when(index == i)
        def _(option=option):
            out_ref[...] = option[...]


def pick(index_of, options):
    shape = options[0].shape
    return pl.pallas_call(
        lambda *refs: pick_kernel(index_of, *refs),
        in_specs=[pl.BlockSpec(memory_space=pltpu.VMEM)] * len(options),
        out_specs=pl.BlockSpec(memory_space=pltpu.VMEM),
        out_shape=jax.ShapeDtypeStruct(shape, jnp.float32),
        compiler_params=grant(1 + (len(options) + 1) * options[0].size * 4 / MIB),
        cost_estimate=pl.CostEstimate(flops=0, bytes_accessed=1 << 19, transcendentals=0),
    )(*options)


def fetch(index, options, out_ref, sem):
    for i, option in enumerate(options):

        @pl.when(index == i)
        def _(option=option):
            copy = pltpu.make_async_copy(option, out_ref, sem)
            copy.start()
            copy.wait()


def fetch_kernel(index_of, *refs):
    fetch(index_of(lax.axis_index("row")), refs[:-2], refs[-2], refs[-1])


def pick_large(index_of, options):
    shape = options[0].shape
    return pl.pallas_call(
        lambda *refs: fetch_kernel(index_of, *refs),
        in_specs=[ANYWHERE] * len(options),
        out_specs=pl.BlockSpec(memory_space=pltpu.VMEM),
        out_shape=jax.ShapeDtypeStruct(shape, jnp.float32),
        scratch_shapes=[pltpu.SemaphoreType.DMA(())],
        compiler_params=grant(4),
        cost_estimate=pl.CostEstimate(flops=0, bytes_accessed=MIB, transcendentals=0),
    )(*options)


def rows_kernel(index_of, *refs):
    options, slab_ref, out_ref, sem = refs[:-3], refs[-3], refs[-2], refs[-1]
    index = index_of(lax.axis_index("row"), lax.axis_index("col"))
    fetch(index, options, out_ref, sem)

    @pl.when(index == len(options))
    def _():
        for h in range(0, slab_ref.shape[1], HALF):
            out_ref[h : h + HALF, :] = slab_ref[:, h : h + HALF].T


def pick_rows(index_of, options, slab):
    shape = options[0].shape
    return pl.pallas_call(
        lambda *refs: rows_kernel(index_of, *refs),
        grid=(1,),
        in_specs=[ANYWHERE] * len(options) + [pl.BlockSpec((PANEL, slab.shape[1]), lambda *_: (0, 0))],
        out_specs=whole(shape),
        out_shape=jax.ShapeDtypeStruct(shape, jnp.float32),
        scratch_shapes=[pltpu.SemaphoreType.DMA(())],
        compiler_params=grant(6),
        cost_estimate=pl.CostEstimate(flops=0, bytes_accessed=2 * MIB, transcendentals=0),
    )(*options, slab)


def partner(c, s, col_size):
    return c ^ s if col_size & (col_size - 1) == 0 else lax.rem(c + s, col_size)


def from_partner(p, c, col_size):
    return c ^ p if col_size & (col_size - 1) == 0 else lax.rem(c - p + col_size, col_size)


def solve_kernel(col_size, ratio, *refs):
    w_ref, rows_ref, pheno_ref = refs[:3]
    lead_refs = refs[3 : 3 + ratio]
    panel_ref = refs[3 + ratio]
    part_refs = refs[4 + ratio : 4 + ratio + col_size]
    inv_ref, head_ref, left_ref = refs[4 + ratio + col_size :]
    row, col = lax.axis_index("row"), lax.axis_index("col")
    member = lax.rem(row, ratio)
    head_share = PANEL // ratio
    traits = head_ref.shape[1]
    for s in range(ratio):
        first = lax.rem(member - s + ratio, ratio) * head_share
        height, width = lead_refs[s].shape
        for i in range(width // traits):
            at = pl.multiple_of(first + i * height, 8)
            head_ref[pl.ds(at, height), :] = lead_refs[s][:, i * traits : (i + 1) * traits]
    full_inverse(w_ref, inv_ref)
    inverse = split(inv_ref[...], 3)
    head = split_dot(inverse, split(head_ref[...], 3), 1, 0)
    panel = split_dot(split(rows_ref[...], 3), inverse, 1, 1)
    panel_ref[...] = panel
    left_ref[...] = pheno_ref[...] - split_dot(split(panel, 2), split(head, 2), 1, 0)

    @pl.when(row == 0)
    def _():
        left_ref[:PANEL, :] = head

    share = left_ref.shape[0] // col_size
    for s in range(col_size):
        at = pl.multiple_of(partner(col, s, col_size) * share, share)
        part_refs[s][...] = left_ref[pl.ds(at, share), :]


def solve_rows(blocks, rows, pheno, slabs, col_size):
    n, traits = pheno.shape
    ratio = len(slabs)
    height = slabs[0].shape[0] - PANEL
    part = jax.ShapeDtypeStruct((n // col_size, traits), jnp.float32)
    lead = pl.BlockSpec((height, slabs[0].shape[1]), lambda *_: (PANEL // height, 0))
    outs = [jax.ShapeDtypeStruct(rows.shape, jnp.float32)] + [part] * col_size
    return pl.pallas_call(
        lambda *refs: solve_kernel(col_size, ratio, *refs),
        grid=(1,),
        in_specs=[whole(blocks.shape), whole(rows.shape), whole(pheno.shape)] + [lead] * ratio,
        out_specs=[whole(o.shape) for o in outs],
        out_shape=outs,
        scratch_shapes=[
            pltpu.VMEM((PANEL, PANEL), jnp.float32),
            pltpu.VMEM((PANEL, traits), jnp.float32),
            pltpu.VMEM(pheno.shape, jnp.float32),
        ],
        compiler_params=grant(12),
        cost_estimate=pl.CostEstimate(flops=1 << 30, bytes_accessed=1 << 21, transcendentals=0),
    )(blocks, rows, pheno, *slabs)


def trailing_kernel(ratio, *refs):
    w_ref, panel_ref, cov_ref = refs[:3]
    slab_refs = refs[3 : 3 + ratio]
    out_ref, inv_ref, high_ref, low_ref = refs[3 + ratio :]
    row, col = lax.axis_index("row"), lax.axis_index("col")
    member = lax.rem(row, ratio)
    step = pl.program_id(0)

    @pl.when(step == 0)
    def _():
        full_inverse(w_ref, inv_ref)
        inverse = split(inv_ref[...], 3)
        for s in range(ratio):
            piece = slab_refs[s].shape[1]
            first = lax.rem(member - s + ratio, ratio) * piece
            for h in range(0, piece, PANEL):
                right = split_dot(inverse, split(slab_refs[s][:, h : h + PANEL], 3), 1, 0)
                at = pl.ds(pl.multiple_of(first + h, PANEL), PANEL)
                high_ref[:, at], low_ref[:, at] = split(right, 2)

    panel = panel_ref[...]
    lead = (row == 0) & (step * panel.shape[0] < PANEL)
    below = jnp.where(lead, 0.0, panel)
    right = [high_ref[...], low_ref[...]]
    out_ref[...] = cov_ref[...] - split_dot(split(below, 2), right, 1, 0)

    @pl.when(col == 0)
    def _():
        out_ref[:, :PANEL] = panel


def trailing_update(blocks, panel, covariance, slabs):
    n, width = covariance.shape
    ratio = len(slabs)
    tall = min(n, PANEL)
    slab = pl.BlockSpec((PANEL, slabs[0].shape[1]), lambda i: (0, 0))
    return pl.pallas_call(
        lambda *refs: trailing_kernel(ratio, *refs),
        grid=(n // tall,),
        in_specs=[
            whole(blocks.shape),
            pl.BlockSpec((tall, PANEL), lambda i: (i, 0)),
            pl.BlockSpec((tall, width), lambda i: (i, 0)),
        ]
        + [slab] * ratio,
        out_specs=pl.BlockSpec((tall, width), lambda i: (i, 0)),
        out_shape=jax.ShapeDtypeStruct(covariance.shape, jnp.float32),
        scratch_shapes=[
            pltpu.VMEM((PANEL, PANEL), jnp.float32),
            pltpu.VMEM((PANEL, width), jnp.bfloat16),
            pltpu.VMEM((PANEL, width), jnp.bfloat16),
        ],
        compiler_params=grant(16),
        cost_estimate=pl.CostEstimate(flops=1 << 31, bytes_accessed=6 << 20, transcendentals=0),
    )(blocks, panel, covariance, *slabs)


def tree(nodes, level, levels, edges):
    if len(nodes) < 2:
        return
    half = len(nodes) // 2
    edges.append((level, levels[nodes[0]], nodes[0], nodes[half]))
    levels[nodes[half]] = level
    tree(nodes[:half], level + 1, levels, edges)
    tree(nodes[half:], level + 1, levels, edges)


def bit_reversed(count):
    bits = max(count - 1, 0).bit_length()
    order = [int(format(i, "0%db" % bits)[::-1], 2) if bits else 0 for i in range(1 << bits)]
    return [i for i in order if i < count]


def choose(index, options):
    out = options[0]
    for i in range(1, len(options)):
        out = jnp.where(index == i, options[i], out)
    return out


def look_up(table, at):
    out = table[0]
    for i, value in enumerate(table):
        if value != table[0]:
            out = jnp.where(at == i, value, out)
    return out


def shards(covariance, phenotypes):
    row_size, col_size = lax.axis_size("row"), lax.axis_size("col")
    row_index, col_index = lax.axis_index("row"), lax.axis_index("col")
    ratio = row_size // col_size
    groups = row_size // ratio
    member = lax.rem(row_index, ratio)

    def place(r, c):
        return r * col_size + c

    def send(x, pairs):
        return lax.ppermute(x, AXES, [(place(*a), place(*b)) for a, b in pairs])

    every_group = [(k, c) for k in range(groups) for c in range(col_size)]

    blocks, *pieces, own_rows = cut(covariance, phenotypes, ratio)
    diag = [blocks]
    for c in range(1, col_size):
        diag.append(send(blocks, [((0, 0), (0, c))]))

    start = [pieces[0]]
    for m in range(1, ratio):
        start.append(send(pieces[m], [((0, c), (m, c)) for c in range(col_size)]))
    start = pick_large(lambda row: jnp.minimum(row, ratio - 1), start)
    stages = {}
    came = {}
    for m in range(ratio):
        nodes = list(range(groups)) if m % 2 == 0 else bit_reversed(groups)
        found = []
        tree(nodes, 1, {0: 0}, found)
        for lv, sl, a, b in found:
            stages.setdefault((lv, sl), []).append((a * ratio + m, b * ratio + m))
            came[b * ratio + m] = (lv, sl)
    keys = sorted(stages)
    results = [start]
    held = {0: start}
    for key in keys:
        pairs = [((a, c), (b, c)) for a, b in stages[key] for c in range(col_size)]
        got = send(held[key[1]], pairs)
        results.append(got)
        if key[0] in held:
            here = [int(came.get(r) == key) for r in range(row_size)]
            held[key[0]] = jnp.where(look_up(here, row_index) > 0, got, held[key[0]])
        else:
            held[key[0]] = got
    source = [keys.index(came[r]) + 1 if r in came else 0 for r in range(row_size)]

    relay_from = col_size // 2
    targets = []
    for r in range(row_size):
        k = r // ratio
        if k:
            line = [c for c in range(1, col_size) if c != k]
        else:
            line = [relay_from] + [c for c in range(1, col_size - 1) if c != relay_from]
        targets.append(line)
    arrived = []
    for j in range(col_size - 2):
        arrived.append(send(own_rows, [((r, 0), (r, targets[r][j])) for r in range(row_size) if j < len(targets[r])]))

    inverse = factor_inverse(diag)
    got = [inverse]
    for k in range(1, groups):
        got.append(send(inverse, [((0, c), (k * ratio, c)) for c in range(col_size)]))
    inverse = pick(lambda row: row // ratio, got)

    arrived.append(send(arrived[0], [((r, relay_from), (r, col_size - 1)) for r in range(ratio)]))
    mine = pick_large(lambda row: look_up(source, row), results)
    slabs = [mine]
    for s in range(1, ratio):
        slabs.append(
            send(
                mine,
                [((k * ratio + m, c), (k * ratio + (m + s) % ratio, c)) for k, c in every_group for m in range(ratio)],
            )
        )

    def index_of(row, col):
        k = row // ratio
        first = jnp.where(
            col == relay_from,
            1,
            jnp.where(col == col_size - 1, col_size - 1, jnp.where(col < relay_from, col + 1, col)),
        )
        later = jnp.where(col == k, col_size, jnp.where(col < k, col, col - 1))
        return jnp.where(col == 0, 0, jnp.where(k == 0, first, later))

    panel_raw = pick_rows(index_of, [own_rows] + arrived, mine)

    got = [inverse]
    for m in range(1, ratio):
        got.append(send(inverse, [((k * ratio, c), (k * ratio + m, c)) for k, c in every_group]))
    inverse = pick(lambda row: lax.rem(row, ratio), got)

    panel, *parts = solve_rows(inverse, panel_raw, phenotypes, slabs, col_size)
    gathered = [parts[0]]
    for s in range(1, col_size):
        pairs = [((r, c), (r, int(partner(c, s, col_size)))) for r in range(row_size) for c in range(col_size)]
        gathered.append(send(parts[s], pairs))
    updated = trailing_update(inverse, panel, covariance, slabs)
    solved = jnp.concatenate(
        [choose(from_partner(p, col_index, col_size), gathered) for p in range(col_size)], axis=1
    )
    return (updated, solved)


def solution(mesh):
    placed = (P("row", "col"), P("row", "col"))

    return jax.shard_map(
        shards,
        mesh=mesh,
        in_specs=placed,
        out_specs=(P("row", "col"), P(("row", "col"), None)),
        check_vma=False,
    )
```

```python
import jax
import jax.numpy as jnp
from jax import lax
from jax.experimental import pallas as pl
from jax.experimental.pallas import tpu as pltpu
from jax.sharding import PartitionSpec as P


PANEL = 256
HALF = PANEL // 2
PIVOTS = 8
EXACT = lax.Precision.HIGHEST
AXES = ("row", "col")


MIB = 1 << 20
ANYWHERE = pl.BlockSpec(memory_space=pl.ANY)
IN_PLACE = pl.BlockSpec(memory_space=pltpu.HBM)
IN_VMEM = pl.BlockSpec(memory_space=pltpu.VMEM)


def grant(mib):
    return pltpu.CompilerParams(vmem_limit_bytes=int(mib * MIB))


def exact_dot(a, b, ca, cb):
    return lax.dot_general(
        a, b, (((ca,), (cb,)), ((), ())), precision=EXACT, preferred_element_type=jnp.float32
    )


def split(x, terms):
    out = []
    for _ in range(terms):
        out.append(x.astype(jnp.bfloat16))
        x = x - out[-1].astype(jnp.float32)
    return out


def split_dot(a, b, ca, cb):
    total = None
    for order in reversed(range(len(a))):
        for i in range(order + 1):
            part = lax.dot_general(
                a[i], b[order - i], (((ca,), (cb,)), ((), ())), preferred_element_type=jnp.float32
            )
            total = part if total is None else total + part
    return total


def eliminate(block, out_ref):
    n = block.shape[0]
    shape = (PIVOTS, n)
    lane = lax.broadcasted_iota(jnp.int32, shape, 1)
    sub = lax.broadcasted_iota(jnp.int32, shape, 0)
    steps = n // PIVOTS

    def spread(x, k):
        return jnp.broadcast_to(x[:, k : k + 1], shape)

    def row_of(x, i):
        return jnp.broadcast_to(x[i : i + 1, :], shape)

    t = [block[PIVOTS * h : PIVOTS * (h + 1), :] for h in range(steps)]
    pivots = [spread(t[0], j) for j in range(PIVOTS)]
    for g in range(steps):
        k0 = g * PIVOTS
        more = g + 1 < steps
        inside = (lane >= k0) & (lane < k0 + PIVOTS)
        e = [[row_of(pivots[j], i) for j in range(i + 1)] for i in range(PIVOTS)]
        r = [
            jnp.where(inside, jnp.where(lane == k0 + k, 1.0, 0.0), row_of(t[g], k))
            for k in range(PIVOTS)
        ]
        if more:
            c = [spread(t[g + 1], k0 + j) for j in range(PIVOTS)]
            following = [spread(t[g + 1], k0 + PIVOTS + j) for j in range(PIVOTS)]
            rows = jnp.where(inside, 0.0, t[g + 1])
        inv = []
        low = [[None] * PIVOTS for _ in range(PIVOTS)]
        for k in range(PIVOTS):
            inv.append(1.0 / e[k][k])
            for i in range(k + 1, PIVOTS):
                low[i][k] = e[i][k] * inv[k]
                for j in range(k + 1, i + 1):
                    e[i][j] = e[i][j] - low[i][k] * e[j][k]
                r[i] = r[i] - low[i][k] * r[k]
            if more:
                f = c[k] * inv[k]
                for j in range(k + 1, PIVOTS):
                    c[j] = c[j] - f * e[j][k]
                rows = rows - f * r[k]
                for j in range(PIVOTS):
                    following[j] = following[j] - f * row_of(c[k], j)
        done = jnp.zeros(shape, jnp.float32)
        for k in range(PIVOTS):
            done = jnp.where(sub == k, r[k] * lax.rsqrt(e[k][k]), done)
        out_ref[k0 : k0 + PIVOTS, :] = jnp.where(lane < k0 + PIVOTS, done, 0.0)
        if not more:
            break
        t[g + 1] = rows
        pivots = following
        if g + 2 < steps:
            q = [r[k] * inv[k] for k in range(PIVOTS)]
            for k in range(PIVOTS - 1, 0, -1):
                for j in range(k):
                    q[j] = q[j] - low[k][j] * q[k]
            for h in range(g + 2, steps):
                acc = jnp.where(inside, 0.0, t[h])
                for j in range(PIVOTS):
                    acc = acc - spread(t[h], k0 + j) * q[j]
                t[h] = acc


def factor_kernel(*refs):
    options, (w_ref, d_ref, w11_ref, w22_ref, sem) = refs[:-5], refs[-5:]
    fetch(lax.axis_index("col"), options, d_ref, sem)
    m = d_ref.shape[0]
    eliminate(d_ref[:, :m], w11_ref)
    w11 = w11_ref[...]
    l21 = exact_dot(d_ref[:, m : 2 * m], w11, 1, 1)
    rest = d_ref[:, 2 * m :] - exact_dot(l21, l21, 1, 1)
    below = exact_dot(l21, w11, 1, 0)
    eliminate(rest, w22_ref)
    w22 = w22_ref[...]
    w_ref[:, :m] = w11
    w_ref[:, m : 2 * m] = -exact_dot(w22, below, 1, 0)
    w_ref[:, 2 * m :] = w22


def factor_inverse(options):
    shape = options[0].shape
    square = pltpu.VMEM((shape[0], shape[0]), jnp.float32)
    return pl.pallas_call(
        factor_kernel,
        in_specs=[ANYWHERE] * len(options),
        out_shape=jax.ShapeDtypeStruct(shape, jnp.float32),
        scratch_shapes=[pltpu.VMEM(shape, jnp.float32), square, square, pltpu.SemaphoreType.DMA(())],
        compiler_params=grant(4),
        cost_estimate=pl.CostEstimate(flops=1 << 32, bytes_accessed=1 << 19, transcendentals=0),
    )(*options)


def full_inverse(w_ref, out_ref):
    m = w_ref.shape[0]
    out_ref[:m, :m] = w_ref[:, :m]
    out_ref[:m, m:] = jnp.zeros((m, m), jnp.float32)
    out_ref[m:, :] = w_ref[:, m:]


def cut_kernel(ratio, cov_ref, pheno_ref, lead_ref, *refs):
    out_refs, (rows_ref, top_ref, rest_ref, head_ref, sem) = refs[:ratio], refs[ratio:]
    piece = out_refs[0].shape[1]
    below = rest_ref.shape[0]
    copies = [
        pltpu.make_async_copy(pheno_ref.at[pl.ds(0, PANEL), :], head_ref, sem.at[0]),
        pltpu.make_async_copy(cov_ref.at[:, pl.ds(0, PANEL)], rows_ref, sem.at[1]),
    ]
    for m in range(ratio):
        source = cov_ref.at[pl.ds(0, PANEL), pl.ds(m * piece, piece)]
        copies.append(pltpu.make_async_copy(source, out_refs[m].at[pl.ds(0, PANEL), :], sem.at[2 + m]))
    for i, (r, c) in enumerate(((0, 0), (1, 0), (1, 1))):
        source = cov_ref.at[pl.ds(r * HALF, HALF), pl.ds(c * HALF, HALF)]
        target = lead_ref.at[:, pl.ds(i * HALF, HALF)]
        copies.append(pltpu.make_async_copy(source, target, sem.at[2 + ratio + i]))
    for i, (first, count, target) in enumerate(((0, PANEL, top_ref), (PANEL, below, rest_ref))):
        source = cov_ref.at[pl.ds(first, count), pl.ds(0, PANEL)]
        copies.append(pltpu.make_async_copy(source, target, sem.at[5 + ratio + i]))
    for copy in copies:
        copy.start()
    copies[0].wait()
    traits = head_ref.shape[1]
    height = out_refs[0].shape[0] - PANEL
    at = 0
    for m in range(ratio):
        for i in range(piece // traits):
            out_refs[m][PANEL:, i * traits : (i + 1) * traits] = head_ref[at : at + height, :]
            at += height
    for copy in copies[1:]:
        copy.wait()


def cut(covariance, phenotypes, ratio):
    n, width = covariance.shape
    traits = phenotypes.shape[1]
    piece = width // ratio
    height = PANEL // ratio // (piece // traits)
    out = jax.ShapeDtypeStruct((PANEL + height, piece), jnp.float32)
    return pl.pallas_call(
        lambda *refs: cut_kernel(ratio, *refs),
        in_specs=[IN_PLACE] * 2,
        out_specs=[IN_VMEM] * (4 + ratio),
        out_shape=[jax.ShapeDtypeStruct((HALF, 3 * HALF), jnp.float32)]
        + [out] * ratio
        + [jax.ShapeDtypeStruct((rows, PANEL), jnp.float32) for rows in (n, PANEL, n - PANEL)],
        scratch_shapes=[pltpu.VMEM((PANEL, traits), jnp.float32), pltpu.SemaphoreType.DMA((7 + ratio,))],
        compiler_params=grant(8),
        cost_estimate=pl.CostEstimate(flops=0, bytes_accessed=4 * MIB, transcendentals=0),
    )(covariance, phenotypes)


def pick_kernel(index_of, *refs):
    options, out_ref = refs[:-1], refs[-1]
    index = index_of(lax.axis_index("row"))
    for i, option in enumerate(options):

        @pl.when(index == i)
        def _(option=option):
            out_ref[...] = option[...]


def pick(index_of, options):
    shape = options[0].shape
    return pl.pallas_call(
        lambda *refs: pick_kernel(index_of, *refs),
        in_specs=[IN_VMEM] * len(options),
        out_specs=IN_VMEM,
        out_shape=jax.ShapeDtypeStruct(shape, jnp.float32),
        compiler_params=grant(1 + (len(options) + 1) * options[0].size * 4 / MIB),
        cost_estimate=pl.CostEstimate(flops=0, bytes_accessed=1 << 19, transcendentals=0),
    )(*options)


def fetch(index, options, out_ref, sem):
    for i, option in enumerate(options):

        @pl.when(index == i)
        def _(option=option):
            copy = pltpu.make_async_copy(option, out_ref, sem)
            copy.start()
            copy.wait()


def fetch_kernel(index_of, *refs):
    fetch(index_of(lax.axis_index("row")), refs[:-2], refs[-2], refs[-1])


def pick_large(index_of, options):
    shape = options[0].shape
    return pl.pallas_call(
        lambda *refs: fetch_kernel(index_of, *refs),
        in_specs=[ANYWHERE] * len(options),
        out_specs=IN_VMEM,
        out_shape=jax.ShapeDtypeStruct(shape, jnp.float32),
        scratch_shapes=[pltpu.SemaphoreType.DMA(())],
        compiler_params=grant(4),
        cost_estimate=pl.CostEstimate(flops=0, bytes_accessed=MIB, transcendentals=0),
    )(*options)


def rows_kernel(index_of, count, *refs):
    tops, rests, (slab_ref, out_ref, sem) = refs[:count], refs[count : 2 * count], refs[2 * count :]
    index = index_of(lax.axis_index("row"), lax.axis_index("col"))
    top_ref, rest_ref = out_ref.at[:PANEL, :], out_ref.at[PANEL:, :]
    for i, (top, rest) in enumerate(zip(tops, rests)):

        @pl.when(index == i)
        def _(top=top, rest=rest):
            if top.shape[0] > PANEL:
                top, rest = top.at[:PANEL, :], rest.at[PANEL:, :]
            copies = [
                pltpu.make_async_copy(top, top_ref, sem.at[0]),
                pltpu.make_async_copy(rest, rest_ref, sem.at[1]),
            ]
            for copy in copies:
                copy.start()
            for copy in copies:
                copy.wait()

    @pl.when(index == count)
    def _():
        for h in range(0, slab_ref.shape[1], HALF):
            out_ref[h : h + HALF, :] = slab_ref[:PANEL, h : h + HALF].T


def pick_rows(index_of, options, slab):
    tops = [option[0] for option in options]
    rests = [option[-1] for option in options]
    shape = (slab.shape[1], PANEL)
    return pl.pallas_call(
        lambda *refs: rows_kernel(index_of, len(options), *refs),
        in_specs=[ANYWHERE] * (2 * len(options)) + [IN_VMEM],
        out_specs=IN_VMEM,
        out_shape=jax.ShapeDtypeStruct(shape, jnp.float32),
        scratch_shapes=[pltpu.SemaphoreType.DMA((2,))],
        compiler_params=grant(4),
        cost_estimate=pl.CostEstimate(flops=0, bytes_accessed=2 * MIB, transcendentals=0),
    )(*tops, *rests, slab)


def partner(c, s, col_size):
    return c ^ s if col_size & (col_size - 1) == 0 else lax.rem(c + s, col_size)


def from_partner(p, c, col_size):
    return c ^ p if col_size & (col_size - 1) == 0 else lax.rem(c - p + col_size, col_size)


def solve_kernel(col_size, ratio, *refs):
    w_ref, rows_ref, pheno_ref = refs[:3]
    lead_refs = refs[3 : 3 + ratio]
    panel_ref = refs[3 + ratio]
    part_refs = refs[4 + ratio : 4 + ratio + col_size]
    inv_ref, head_ref, left_ref = refs[4 + ratio + col_size :]
    row, col = lax.axis_index("row"), lax.axis_index("col")
    member = lax.rem(row, ratio)
    head_share = PANEL // ratio
    traits = head_ref.shape[1]
    for s in range(ratio):
        first = lax.rem(member - s + ratio, ratio) * head_share
        height, width = lead_refs[s].shape[0] - PANEL, lead_refs[s].shape[1]
        for i in range(width // traits):
            at = pl.multiple_of(first + i * height, 8)
            head_ref[pl.ds(at, height), :] = lead_refs[s][PANEL:, i * traits : (i + 1) * traits]
    full_inverse(w_ref, inv_ref)
    inverse = split(inv_ref[...], 3)
    head = split_dot(inverse, split(head_ref[...], 3), 1, 0)
    panel = split_dot(split(rows_ref[...], 3), inverse, 1, 1)
    panel_ref[...] = panel
    left_ref[...] = pheno_ref[...] - split_dot(split(panel, 2), split(head, 2), 1, 0)

    @pl.when(row == 0)
    def _():
        left_ref[:PANEL, :] = head

    share = left_ref.shape[0] // col_size
    for s in range(col_size):
        at = pl.multiple_of(partner(col, s, col_size) * share, share)
        part_refs[s][...] = left_ref[pl.ds(at, share), :]


def solve_rows(blocks, rows, pheno, slabs, col_size):
    n, traits = pheno.shape
    ratio = len(slabs)
    part = jax.ShapeDtypeStruct((n // col_size, traits), jnp.float32)
    outs = [jax.ShapeDtypeStruct(rows.shape, jnp.float32)] + [part] * col_size
    return pl.pallas_call(
        lambda *refs: solve_kernel(col_size, ratio, *refs),
        in_specs=[IN_VMEM] * (3 + ratio),
        out_specs=[IN_VMEM] * len(outs),
        out_shape=outs,
        scratch_shapes=[
            pltpu.VMEM((PANEL, PANEL), jnp.float32),
            pltpu.VMEM((PANEL, traits), jnp.float32),
            pltpu.VMEM(pheno.shape, jnp.float32),
        ],
        compiler_params=grant(12),
        cost_estimate=pl.CostEstimate(flops=1 << 30, bytes_accessed=1 << 21, transcendentals=0),
    )(blocks, rows, pheno, *slabs)


def trailing_kernel(ratio, *refs):
    w_ref, panel_ref, cov_ref = refs[:3]
    slab_refs = refs[3 : 3 + ratio]
    out_ref, inv_ref, high_ref, low_ref = refs[3 + ratio :]
    row, col = lax.axis_index("row"), lax.axis_index("col")
    member = lax.rem(row, ratio)
    step = pl.program_id(0)

    @pl.when(step == 0)
    def _():
        full_inverse(w_ref, inv_ref)
        inverse = split(inv_ref[...], 3)
        for s in range(ratio):
            piece = slab_refs[s].shape[1]
            first = lax.rem(member - s + ratio, ratio) * piece
            for h in range(0, piece, PANEL):
                right = split_dot(inverse, split(slab_refs[s][:PANEL, h : h + PANEL], 3), 1, 0)
                at = pl.ds(pl.multiple_of(first + h, PANEL), PANEL)
                high_ref[:, at], low_ref[:, at] = split(right, 2)

    panel = panel_ref[...]
    lead = (row == 0) & (step * panel.shape[0] < PANEL)
    below = jnp.where(lead, 0.0, panel)
    right = [high_ref[...], low_ref[...]]
    out_ref[...] = cov_ref[...] - split_dot(split(below, 2), right, 1, 0)

    @pl.when(col == 0)
    def _():
        out_ref[:, :PANEL] = panel


def trailing_update(blocks, panel, covariance, slabs):
    n, width = covariance.shape
    ratio = len(slabs)
    tall = min(n, PANEL)
    return pl.pallas_call(
        lambda *refs: trailing_kernel(ratio, *refs),
        grid=(n // tall,),
        in_specs=[
            IN_VMEM,
            pl.BlockSpec((tall, PANEL), lambda i: (i, 0)),
            pl.BlockSpec((tall, width), lambda i: (i, 0)),
        ]
        + [IN_VMEM] * ratio,
        out_specs=pl.BlockSpec((tall, width), lambda i: (i, 0)),
        out_shape=jax.ShapeDtypeStruct(covariance.shape, jnp.float32),
        scratch_shapes=[
            pltpu.VMEM((PANEL, PANEL), jnp.float32),
            pltpu.VMEM((PANEL, width), jnp.bfloat16),
            pltpu.VMEM((PANEL, width), jnp.bfloat16),
        ],
        compiler_params=grant(16),
        cost_estimate=pl.CostEstimate(flops=1 << 31, bytes_accessed=6 << 20, transcendentals=0),
    )(blocks, panel, covariance, *slabs)


def tree(nodes, level, levels, edges):
    if len(nodes) < 2:
        return
    half = len(nodes) // 2
    edges.append((level, levels[nodes[0]], nodes[0], nodes[half]))
    levels[nodes[half]] = level
    tree(nodes[:half], level + 1, levels, edges)
    tree(nodes[half:], level + 1, levels, edges)


def bit_reversed(count):
    bits = max(count - 1, 0).bit_length()
    order = [int(format(i, "0%db" % bits)[::-1], 2) if bits else 0 for i in range(1 << bits)]
    return [i for i in order if i < count]


def choose(index, options):
    out = options[0]
    for i in range(1, len(options)):
        out = jnp.where(index == i, options[i], out)
    return out


def look_up(table, at):
    out = table[0]
    for i, value in enumerate(table):
        if value != table[0]:
            out = jnp.where(at == i, value, out)
    return out


def shards(covariance, phenotypes):
    row_size, col_size = lax.axis_size("row"), lax.axis_size("col")
    row_index, col_index = lax.axis_index("row"), lax.axis_index("col")
    ratio = row_size // col_size
    groups = row_size // ratio
    member = lax.rem(row_index, ratio)

    def place(r, c):
        return r * col_size + c

    def send(x, pairs):
        return lax.ppermute(x, AXES, [(place(*a), place(*b)) for a, b in pairs])

    every_group = [(k, c) for k in range(groups) for c in range(col_size)]

    blocks, *pieces, own_rows, own_top, own_rest = cut(covariance, phenotypes, ratio)
    diag = [blocks]
    for c in range(1, col_size):
        diag.append(send(blocks, [((0, 0), (0, c))]))

    start = [pieces[0]]
    for m in range(1, ratio):
        start.append(send(pieces[m], [((0, c), (m, c)) for c in range(col_size)]))
    start = pick_large(lambda row: jnp.minimum(row, ratio - 1), start)
    stages = {}
    came = {}
    for m in range(ratio):
        nodes = list(range(groups)) if m % 2 == 0 else bit_reversed(groups)
        found = []
        tree(nodes, 1, {0: 0}, found)
        for lv, sl, a, b in found:
            stages.setdefault((lv, sl), []).append((a * ratio + m, b * ratio + m))
            came[b * ratio + m] = (lv, sl)
    keys = sorted(stages)
    results = [start]
    held = {0: start}
    for key in keys:
        pairs = [((a, c), (b, c)) for a, b in stages[key] for c in range(col_size)]
        got = send(held[key[1]], pairs)
        results.append(got)
        if key[0] in held:
            here = [int(came.get(r) == key) for r in range(row_size)]
            held[key[0]] = jnp.where(look_up(here, row_index) > 0, got, held[key[0]])
        else:
            held[key[0]] = got
    source = [keys.index(came[r]) + 1 if r in came else 0 for r in range(row_size)]

    relay_from = col_size // 2
    targets = []
    for r in range(row_size):
        k = r // ratio
        if k:
            line = [c for c in range(1, col_size) if c != k]
        else:
            line = [relay_from] + [c for c in range(1, col_size - 1) if c != relay_from]
        targets.append(line)
    first = [((r, 0), (r, targets[r][0])) for r in range(row_size)]
    arrived = [(send(own_top, first[1:]), send(own_rest, first))]
    for j in range(1, col_size - 2):
        pairs = [((r, 0), (r, targets[r][j])) for r in range(row_size) if j < len(targets[r])]
        arrived.append((send(own_rows, pairs),))

    inverse = factor_inverse(diag)
    got = [inverse]
    for k in range(1, groups):
        got.append(send(inverse, [((0, c), (k * ratio, c)) for c in range(col_size)]))
    inverse = pick(lambda row: row // ratio, got)

    relays = [((r, relay_from), (r, col_size - 1)) for r in range(ratio)]
    arrived.append((send(arrived[0][0], relays[1:]), send(arrived[0][1], relays)))
    mine = pick_large(lambda row: look_up(source, row), results)
    slabs = [mine]
    for s in range(1, ratio):
        slabs.append(
            send(
                mine,
                [((k * ratio + m, c), (k * ratio + (m + s) % ratio, c)) for k, c in every_group for m in range(ratio)],
            )
        )
    slabs = slabs[:1] + [pick_large(lambda row: 0 * row, [slab]) for slab in slabs[1:]]

    def index_of(row, col):
        k = row // ratio
        first = jnp.where(
            col == relay_from,
            1,
            jnp.where(col == col_size - 1, col_size - 1, jnp.where(col < relay_from, col + 1, col)),
        )
        later = jnp.where(col == k, col_size, jnp.where(col < k, col, col - 1))
        return jnp.where(col == 0, 0, jnp.where(k == 0, first, later))

    panel_raw = pick_rows(index_of, [(own_rows,)] + arrived, mine)

    got = [inverse]
    for m in range(1, ratio):
        got.append(send(inverse, [((k * ratio, c), (k * ratio + m, c)) for k, c in every_group]))
    inverse = pick(lambda row: lax.rem(row, ratio), got)

    panel, *parts = solve_rows(inverse, panel_raw, phenotypes, slabs, col_size)
    gathered = [parts[0]]
    for s in range(1, col_size):
        pairs = [((r, c), (r, int(partner(c, s, col_size)))) for r in range(row_size) for c in range(col_size)]
        gathered.append(send(parts[s], pairs))
    updated = trailing_update(inverse, panel, covariance, slabs)
    solved = jnp.concatenate(
        [choose(from_partner(p, col_index, col_size), gathered) for p in range(col_size)], axis=1
    )
    return (updated, solved)


def solution(mesh):
    placed = (P("row", "col"), P("row", "col"))

    return jax.shard_map(
        shards,
        mesh=mesh,
        in_specs=placed,
        out_specs=(P("row", "col"), P(("row", "col"), None)),
        check_vma=False,
    )
```
